128 devices in a mesh: dp: 32 (over x, y_lo, z), grp: 4 (over y_hi, core).
Axes of the slice: x: 4, y: 4 (y_hi: 2, y_lo: 2; y = y_hi * 2 + y_lo), z: 4, core: 2. Of those that a mesh axis runs over, the one named last changes fastest.
Arguments:
- images: bfloat16 [65536, 128, 128], P(('dp', 'grp')), may hold values from -6 to 6
- shifts: int32 [65536, 2], P(('dp', 'grp')), may hold values from -16 to 16
- class_ids: int32 [65536], P(('dp', 'grp')), may hold values from 0 to 255
- next_block: bfloat16 [1024, 2, 4096], P('grp'), may hold values from -6 to 6
Outputs:
- averages: float32 [256, 2, 4096], P(('dp', 'grp'))
- scores: float32 [256, 1024], P('dp', 'grp')
The draws below stay inside these ranges and needn't reach their ends.
All inputs are finite; a program needn't handle non-finite values.
Results may differ from the reference program's by a relative error of at most 0.014.
Values may be sent and summed in bfloat16 or wider, within the bound.
A program may use at most 128 MiB of HBM per device.

```python
import math
import jax
import jax.numpy as jnp
import numpy as np
from jax import lax

PIX = 128
BAND = 64
CLASSES = 256
IMG_DEV = 512
IMAGES = 65536
NEXT = 1024


def with_ends(array, rng, smallest, top_value):
    dims = array.shape
    index_at = [jax.random.randint(jax.random.fold_in(rng, axis), (), 0, dims[axis]) for axis in range(len(dims))]
    array = array.at[tuple(index_at)].set(smallest)
    longest = dims.index(max(dims))
    index_at[longest] = (index_at[longest] + 1) % dims[longest]
    return array.at[tuple(index_at)].set(top_value)


def steps_of(rng, dims, shards, least, largest):
    def one(position, shards_of):
        heights = jax.random.uniform(jax.random.fold_in(jax.random.fold_in(rng, 6), position), (shards_of,), jnp.float32, least / len(shards), largest / len(shards))
        return jnp.repeat(jnp.exp(heights), dims[position] // shards_of).reshape((-1,) + (1,) * (len(dims) - position - 1))

    factor_of = one(*shards[0])
    for cut in shards[1:]:
        factor_of = factor_of * one(*cut)
    return factor_of


def cumulative_ranks(amount, lean):
    weights = [(1 << 20) // math.isqrt(standing ** lean) + 1 for standing in range(1, amount + 1)]
    spread = 1 + sum(weights) // (1 << 30)
    return np.cumsum(np.array([max(1, weight // spread) for weight in weights]))


def ranked(stream_key, extent, count, skew):
    listing = cumulative_ranks(count, skew)
    lot = jax.random.randint(jax.random.fold_in(stream_key, 1), extent, 0, int(listing[count - 1]))
    rank = jnp.searchsorted(jnp.asarray(listing, jnp.int32), lot, side="right")
    return jax.random.permutation(jax.random.fold_in(stream_key, 2), count)[rank].astype(jnp.int32)


def normal_values(key, dims, spread, reach, pieces=(), held_as=jnp.bfloat16):
    entries = spread * jax.random.normal(key, dims, jnp.float32)
    if pieces:
        entries = entries * steps_of(key, dims, pieces, -0.22, 0.18)
    return jnp.clip(entries, -reach, reach).astype(held_as)


def setup_inputs(seed: int = 0) -> dict:
    streams_of = jax.random.split(jax.random.key(seed), 5)
    return {
        "images": normal_values(streams_of[0], (IMAGES, PIX, PIX), 1.0, 6.0, ((0, 128),)),
        "shifts": with_ends(jax.random.randint(streams_of[1], (IMAGES, 2), -(PIX // 8), PIX // 8 + 1), jax.random.fold_in(streams_of[1], 1), -(PIX // 8), (PIX // 8 + 1) - 1).astype(jnp.int32),
        "class_ids": with_ends(ranked(streams_of[2], (IMAGES,), CLASSES, 1), jax.random.fold_in(streams_of[2], 3), 0, CLASSES - 1).astype(jnp.int32),
        "next_block": normal_values(streams_of[3], (NEXT, 2, BAND * BAND), 1.0, 6.0, ((0, 4),)),
    }


ridge = 4.0

def dft_tables():
    positions = jnp.arange(PIX, dtype=jnp.int32)
    signed_freq = jnp.arange(BAND, dtype=jnp.int32) - BAND // 2
    residue = positions[:, None] * signed_freq[None, :] % PIX
    phase_angle = residue.astype(jnp.float32) * (2.0 * math.pi / PIX)
    scaling = 1.0 / math.sqrt(PIX)
    cosine = (jnp.cos(phase_angle) * scaling).astype(jnp.bfloat16)
    sine = (jnp.sin(phase_angle) * scaling).astype(jnp.bfloat16)
    return (jnp.concatenate([cosine, sine], axis=1), signed_freq)

def band_filter(signed_freq):
    squared = signed_freq.astype(jnp.float32) ** 2
    radius = squared[:, None] + squared[None, :]
    return jnp.exp(-radius / (BAND * BAND / 2.0)).reshape(BAND * BAND)

def shifted_transform(block_imgs, block_shifts, tables, signed_freq):
    num_img = block_imgs.shape[0]
    column_section = jnp.einsum('iyx,xm->iym', block_imgs.astype(jnp.float32), tables.astype(jnp.float32)).astype(jnp.bfloat16)
    row_section = jnp.einsum('yt,iym->itm', tables.astype(jnp.float32), column_section.astype(jnp.float32))
    cos_cos = row_section[:, :BAND, :BAND]
    cos_sin = row_section[:, :BAND, BAND:]
    sin_cos = row_section[:, BAND:, :BAND]
    sin_sin = row_section[:, BAND:, BAND:]
    four_real = cos_cos - sin_sin
    four_imag = -(sin_cos + cos_sin)
    shift_x = block_shifts[:, 0][:, None, None]
    shift_y = block_shifts[:, 1][:, None, None]
    residue = (signed_freq[None, :, None] * shift_y + signed_freq[None, None, :] * shift_x) % PIX
    phase_angle = residue.astype(jnp.float32) * (2.0 * math.pi / PIX)
    ramp_cos = jnp.cos(phase_angle)
    ramp_sin = jnp.sin(phase_angle)
    moved_real = four_real * ramp_cos + four_imag * ramp_sin
    moved_imag = four_imag * ramp_cos - four_real * ramp_sin
    return jnp.stack([moved_real, moved_imag], axis=1).reshape(num_img, 2 * BAND * BAND).astype(jnp.bfloat16)

def reference(images, shifts, class_ids, next_block):
    tables, signed_freq = dft_tables()
    blocks = IMAGES // IMG_DEV
    stacked = (images.reshape(blocks, IMG_DEV, PIX, PIX), shifts.reshape(blocks, IMG_DEV, 2), class_ids.reshape(blocks, IMG_DEV))

    def accumulate(running, item):
        moved = shifted_transform(item[0], item[1], tables, signed_freq)
        added = jax.ops.segment_sum(moved.astype(jnp.float32), item[2], num_segments=CLASSES)
        return (running + added, None)
    class_sum, _ = lax.scan(accumulate, jnp.zeros((CLASSES, 2 * BAND * BAND), jnp.float32), stacked)
    members = jax.ops.segment_sum(jnp.ones((IMAGES,), jnp.float32), class_ids, num_segments=CLASSES)
    averages = class_sum.reshape(CLASSES, 2, BAND * BAND) * band_filter(signed_freq)[None, None, :] / (members + ridge)[:, None, None]
    references = averages.astype(jnp.bfloat16)
    energy = lax.optimization_barrier(jnp.sum(jnp.square(references.astype(jnp.float32)), axis=(1, 2)))
    inner_prod = jnp.dot(references.reshape(CLASSES, 2 * BAND * BAND), next_block.reshape(NEXT, 2 * BAND * BAND).T, preferred_element_type=jnp.float32)
    scores = (inner_prod - 0.5 * energy[:, None]) / BAND
    return (averages, scores)
```

```python
import math

import jax
import jax.numpy as jnp
import numpy as np
from jax import lax
from jax.experimental import pallas as pl
from jax.experimental.pallas import tpu as pltpu
from jax.sharding import PartitionSpec as P

PIX = 128
BAND = 64
CLASSES = 256
REACH = 16
ROWS = PIX + 2 * REACH
OUT_ROWS = 72
STEP = 32
ridge = 4.0


def basis(positions):
    freq = np.concatenate([np.arange(32), np.arange(1, 32), [32, 32]])
    angle = (positions[:, None] * freq[None, :] % PIX) * (2.0 * math.pi / PIX)
    is_sin = np.zeros(65, bool)
    is_sin[32:63] = True
    is_sin[64] = True
    return np.where(is_sin[None, :], np.sin(angle), np.cos(angle)) / math.sqrt(PIX)


def constants():
    bx = basis(np.arange(PIX))
    by = basis(np.arange(ROWS) - REACH)
    w1 = np.zeros((256, 256))
    w1[:128, :64] = bx[:, :64]
    w1[128:, 64:128] = bx[:, :64]
    w1[:128, 128::2] = bx[:, 64:]
    w1[128:, 129::2] = bx[:, 64:]
    by_rows = np.zeros((OUT_ROWS, ROWS))
    by_rows[:65] = by.T
    by_cols = np.zeros((ROWS, 128))
    by_cols[:, :65] = by
    return [jnp.asarray(a.astype(np.float32), jnp.bfloat16) for a in (w1, by_rows, by_cols)]


def selections():
    freq = np.arange(BAND) - BAND // 2
    size = np.abs(freq)
    cos_at = np.where(size == 32, 63, size)
    sin_at = np.where(size == 32, 64, 31 + size)
    sign = np.sign(freq)
    yc = np.zeros((BAND, 128))
    ys = np.zeros((BAND, 128))
    yc[np.arange(BAND), cos_at] = 1.0
    ys[np.arange(BAND), sin_at] = sign
    ys[size == 0] = 0.0
    ysel = np.concatenate([yc, ys], axis=0)
    xc = np.zeros((128, 128))
    xs = np.zeros((128, 128))
    for j in range(2):
        xc[64 * j : 64 * j + 64, 64 * j : 64 * j + 64] = yc[:, :64].T
        xs[64 * j : 64 * j + 64, 64 * j : 64 * j + 64] = ys[:, :64].T
    return ysel, xc, xs


def partial_kernel(code_ref, img_ref, ids_ref, w1_ref, byr_ref, byc_ref, out_ref, acc, x2, edge):
    step = pl.program_id(0)

    @pl.when(step == 0)
    def _():
        def clear(c, carry):
            acc[c] = jnp.zeros((ROWS, PIX), jnp.float32)
            return carry

        lax.fori_loop(0, CLASSES, clear, 0)

    def add_image(i, carry):
        code = code_ref[step * STEP + i]
        cls = code >> 13
        row = (code >> 7) & 63
        moved = pltpu.roll(img_ref[i].astype(jnp.float32), code & 127, 1)
        acc[cls, pl.ds(row, PIX), :] += moved
        return carry

    lax.fori_loop(0, STEP, add_image, 0, unroll=4)

    @pl.when(step == pl.num_programs(0) - 1)
    def _():
        lane_pair = lax.broadcasted_iota(jnp.int32, (ROWS, 128), 1) // 2
        for half in range(2):

            def columns(p, held):
                pair = half * 64 + p
                lhs = jnp.concatenate([acc[2 * pair], acc[2 * pair + 1]], axis=1)
                got = jnp.dot(
                    lhs.astype(jnp.bfloat16), w1_ref[...], preferred_element_type=jnp.float32
                )
                x2[pair] = got[:, :128].astype(jnp.bfloat16)
                return jnp.where(lane_pair == p, got[:, 128:], held)

            held = lax.fori_loop(0, 64, columns, jnp.zeros((ROWS, 128), jnp.float32), unroll=2)
            edge[:, half * 128 : half * 128 + 128] = held.astype(jnp.bfloat16)
        side = lax.dot_general(
            edge[...], byc_ref[...], (((0,), (0,)), ((), ())), preferred_element_type=jnp.float32
        )
        count = jnp.sum(
            jnp.where(
                lax.broadcasted_iota(jnp.int32, (CLASSES, ids_ref.shape[1]), 0) == ids_ref[...],
                1.0,
                0.0,
            ),
            axis=1,
            keepdims=True,
        ).astype(jnp.int32)
        lane = lax.broadcasted_iota(jnp.int32, (CLASSES, 128), 1)
        bit = lane - 65
        tally = jnp.where(
            (bit >= 0) & (bit < 12), (count >> jnp.clip(bit, 0, 12)) & 1, 0
        ).astype(jnp.float32)
        acc[0, 0:128, :] = side[:128] + tally[:128]
        acc[1, 0:128, :] = side[128:] + tally[128:]

        def rows(q2, carry):
            eight = acc[q2 // 16, pl.ds(pl.multiple_of((q2 % 16) * 8, 8), 8), :]
            sub = lax.broadcasted_iota(jnp.int32, (8, 128), 0)
            place = (sub == 1) | (sub == 2)
            for k in range(2):
                q = q2 * 2 + k
                rhs = jnp.concatenate([x2[2 * q], x2[2 * q + 1]], axis=1)
                got = jnp.dot(byr_ref[...], rhs, preferred_element_type=jnp.float32)
                for core in range(2):
                    part = got[:, 128 * core : 128 * core + 128]
                    at = 4 * k + 2 * core
                    extra = jnp.where(place, pltpu.roll(eight, (1 - at) % 8, 0), 0.0)
                    out_ref[core, q, 0:64, :] = part[:64].astype(jnp.bfloat16)
                    out_ref[core, q, 64:72, :] = (part[64:] + extra).astype(jnp.bfloat16)
            return carry

        lax.fori_loop(0, 32, rows, 0, unroll=2)


def partial_sums(images, code, ids):
    count = images.shape[0]
    w1, byr, byc = constants()
    whole = lambda a: pl.BlockSpec(a.shape, lambda i, c: (0,) * a.ndim)
    out = jax.ShapeDtypeStruct((2, 64, OUT_ROWS, 128), jnp.bfloat16)
    return pl.pallas_call(
        partial_kernel,
        out_shape=out,
        grid_spec=pltpu.PrefetchScalarGridSpec(
            num_scalar_prefetch=1,
            grid=(count // STEP,),
            in_specs=[
                pl.BlockSpec((STEP, PIX, PIX), lambda i, c: (i, 0, 0)),
                whole(ids),
                whole(w1),
                whole(byr),
                whole(byc),
            ],
            out_specs=pl.BlockSpec(out.shape, lambda i, c: (0, 0, 0, 0)),
            scratch_shapes=[
                pltpu.VMEM((CLASSES, ROWS, PIX), jnp.float32),
                pltpu.VMEM((128, ROWS, 128), jnp.bfloat16),
                pltpu.VMEM((ROWS, 256), jnp.bfloat16),
            ],
        ),
        compiler_params=pltpu.CompilerParams(
            dimension_semantics=("arbitrary",), vmem_limit_bytes=48 << 20
        ),
        name="partial_sums",
    )(code, images, ids, w1, byr, byc)


def band_filter():
    freq = (np.arange(BAND) - BAND // 2).astype(np.float64) ** 2
    return np.exp(-(freq[:, None] + freq[None, :]) / (BAND * BAND / 2.0)).astype(np.float32)


def body(images, shifts, class_ids, next_block):
    code = (class_ids * 64 + shifts[:, 1] + REACH) * 128 + (shifts[:, 0] & (PIX - 1))
    partial = partial_sums(images, code, class_ids[None, :])
    mine = lax.psum_scatter(
        partial.transpose(1, 0, 2, 3).reshape(128, OUT_ROWS * 128).astype(jnp.float32),
        ("dp", "grp"),
        scatter_dimension=0,
        tiled=True,
    ).reshape(OUT_ROWS, 128)
    ysel, xc, xs = (jnp.asarray(a, jnp.float32) for a in selections())
    high = lax.Precision.HIGHEST
    members = jnp.sum(mine[65:67, 65:77] * (2.0 ** jnp.arange(12))[None, :], axis=1)
    yr = jnp.dot(ysel[:, :65], mine[:65], precision=high)
    yt = jnp.dot(ysel[:, :65], mine[65:67, :65].T, precision=high)
    ec, es = yt[:64], yt[64:]
    rc = jnp.dot(yr, xc, precision=high)
    rs = jnp.dot(yr, xs, precision=high)
    four_real = (rc[:64] - rs[64:]).reshape(64, 2, 64).at[:, :, 0].add(es)
    four_imag = -(rc[64:] + rs[:64]).reshape(64, 2, 64).at[:, :, 0].add(-ec)
    class_sum = jnp.stack([four_real, four_imag], axis=0).transpose(2, 0, 1, 3)
    averages = class_sum * band_filter()[None, None] / (members + ridge)[:, None, None, None]
    averages = averages.reshape(2, 2, BAND * BAND)
    references = averages.astype(jnp.bfloat16)
    next_flat = next_block.reshape(next_block.shape[0], 2 * BAND * BAND)
    ref_piece = lax.all_gather(references, "grp", axis=0, tiled=True)
    energy = jnp.sum(jnp.square(ref_piece.astype(jnp.float32)), axis=(1, 2))
    flat_piece = ref_piece.reshape(ref_piece.shape[0], 2 * BAND * BAND)
    inner_prod = lax.dot_general(
        flat_piece, next_flat, (((1,), (1,)), ((), ())), preferred_element_type=jnp.float32
    )
    scores = (inner_prod - 0.5 * energy[:, None]) / BAND
    return (averages, scores)


def solution(mesh):
    placed = (
        P(("dp", "grp"), None, None),
        P(("dp", "grp"), None),
        P(("dp", "grp")),
        P("grp", None, None),
    )
    return jax.shard_map(
        body,
        mesh=mesh,
        in_specs=placed,
        out_specs=(P(("dp", "grp"), None, None), P("dp", "grp")),
        check_vma=False,
    )
```

```python
import math

import jax
import jax.numpy as jnp
import numpy as np
from jax import lax
from jax.experimental import pallas as pl
from jax.experimental.pallas import tpu as pltpu
from jax.sharding import PartitionSpec as P

PIX = 128
BAND = 64
CLASSES = 256
REACH = 16
ROWS = PIX + 2 * REACH
OUT_ROWS = 72
STEP = 32
ridge = 4.0


def basis(positions):
    freq = np.concatenate([np.arange(32), np.arange(1, 32), [32, 32]])
    angle = (positions[:, None] * freq[None, :] % PIX) * (2.0 * math.pi / PIX)
    is_sin = np.zeros(65, bool)
    is_sin[32:63] = True
    is_sin[64] = True
    return np.where(is_sin[None, :], np.sin(angle), np.cos(angle)) / math.sqrt(PIX)


def constants():
    bx = basis(np.arange(PIX))
    by = basis(np.arange(ROWS) - REACH)
    w1 = np.zeros((256, 256))
    w1[:128, :64] = bx[:, :64]
    w1[128:, 64:128] = bx[:, :64]
    w1[:128, 128::2] = bx[:, 64:]
    w1[128:, 129::2] = bx[:, 64:]
    by_rows = np.zeros((OUT_ROWS, ROWS))
    by_rows[:65] = by.T
    by_cols = np.zeros((ROWS, 128))
    by_cols[:, :65] = by
    return [jnp.asarray(a.astype(np.float32), jnp.bfloat16) for a in (w1, by_rows, by_cols)]


def selections():
    freq = np.arange(BAND) - BAND // 2
    size = np.abs(freq)
    cos_at = np.where(size == 32, 63, size)
    sin_at = np.where(size == 32, 64, 31 + size)
    sign = np.sign(freq)
    yc = np.zeros((BAND, 128))
    ys = np.zeros((BAND, 128))
    yc[np.arange(BAND), cos_at] = 1.0
    ys[np.arange(BAND), sin_at] = sign
    ys[size == 0] = 0.0
    ysel = np.concatenate([yc, ys], axis=0)
    xc = np.zeros((128, 128))
    xs = np.zeros((128, 128))
    for j in range(2):
        xc[64 * j : 64 * j + 64, 64 * j : 64 * j + 64] = yc[:, :64].T
        xs[64 * j : 64 * j + 64, 64 * j : 64 * j + 64] = ys[:, :64].T
    return ysel, xc, xs


def partial_kernel(code_ref, img_ref, ids_ref, w1_ref, byr_ref, byc_ref, out_ref, acc, x2, edge):
    step = pl.program_id(0)

    @pl.when(step == 0)
    def _():
        def clear(c, carry):
            acc[c] = jnp.zeros((ROWS, PIX), jnp.float32)
            return carry

        lax.fori_loop(0, CLASSES, clear, 0)

    def add_image(i, carry):
        code = code_ref[step * STEP + i]
        cls = code >> 13
        row = (code >> 7) & 63
        moved = pltpu.roll(img_ref[i].astype(jnp.float32), code & 127, 1)
        acc[cls, pl.ds(row, PIX), :] += moved
        return carry

    lax.fori_loop(0, STEP, add_image, 0, unroll=4)

    @pl.when(step == pl.num_programs(0) - 1)
    def _():
        lane_pair = lax.broadcasted_iota(jnp.int32, (ROWS, 128), 1) // 2
        for half in range(2):

            def columns(p, held):
                pair = half * 64 + p
                lhs = jnp.concatenate([acc[2 * pair], acc[2 * pair + 1]], axis=1)
                got = jnp.dot(
                    lhs.astype(jnp.bfloat16), w1_ref[...], preferred_element_type=jnp.float32
                )
                x2[pair] = got[:, :128].astype(jnp.bfloat16)
                return jnp.where(lane_pair == p, got[:, 128:], held)

            held = lax.fori_loop(0, 64, columns, jnp.zeros((ROWS, 128), jnp.float32), unroll=2)
            edge[:, half * 128 : half * 128 + 128] = held.astype(jnp.bfloat16)
        side = lax.dot_general(
            edge[...], byc_ref[...], (((0,), (0,)), ((), ())), preferred_element_type=jnp.float32
        )
        count = jnp.sum(
            jnp.where(
                lax.broadcasted_iota(jnp.int32, (CLASSES, ids_ref.shape[1]), 0) == ids_ref[...],
                1.0,
                0.0,
            ),
            axis=1,
            keepdims=True,
        ).astype(jnp.int32)
        lane = lax.broadcasted_iota(jnp.int32, (CLASSES, 128), 1)
        bit = lane - 65
        tally = jnp.where(
            (bit >= 0) & (bit < 12), (count >> jnp.clip(bit, 0, 12)) & 1, 0
        ).astype(jnp.float32)
        acc[0, 0:128, :] = side[:128] + tally[:128]
        acc[1, 0:128, :] = side[128:] + tally[128:]

        def rows(q2, carry):
            eight = acc[q2 // 16, pl.ds(pl.multiple_of((q2 % 16) * 8, 8), 8), :]
            sub = lax.broadcasted_iota(jnp.int32, (8, 128), 0)
            place = (sub == 1) | (sub == 2)
            for k in range(2):
                q = q2 * 2 + k
                rhs = jnp.concatenate([x2[2 * q], x2[2 * q + 1]], axis=1)
                got = jnp.dot(byr_ref[...], rhs, preferred_element_type=jnp.float32)
                for core in range(2):
                    part = got[:, 128 * core : 128 * core + 128]
                    at = 4 * k + 2 * core
                    extra = jnp.where(place, pltpu.roll(eight, (1 - at) % 8, 0), 0.0)
                    whole = jnp.concatenate([part[:64], part[64:] + extra], axis=0)
                    x, y, z = q // 16, (q % 2) * 2 + (q // 8) % 2, (q // 2) % 4
                    spots = (x * 16 + y * 4 + z, y * 16 + z * 4 + x, z * 16 + x * 4 + y)
                    for color in range(3):
                        out_ref[core, color, spots[color]] = whole[
                            24 * color : 24 * color + 24
                        ].astype(jnp.bfloat16)
            return carry

        lax.fori_loop(0, 32, rows, 0, unroll=2)


def partial_sums(images, code, ids):
    count = images.shape[0]
    w1, byr, byc = constants()
    whole = lambda a: pl.BlockSpec(a.shape, lambda i, c: (0,) * a.ndim)
    out = jax.ShapeDtypeStruct((2, 3, 64, 24, 128), jnp.bfloat16)
    return pl.pallas_call(
        partial_kernel,
        out_shape=out,
        grid_spec=pltpu.PrefetchScalarGridSpec(
            num_scalar_prefetch=1,
            grid=(count // STEP,),
            in_specs=[
                pl.BlockSpec((STEP, PIX, PIX), lambda i, c: (i, 0, 0)),
                whole(ids),
                whole(w1),
                whole(byr),
                whole(byc),
            ],
            out_specs=pl.BlockSpec(out.shape, lambda i, c: (0, 0, 0, 0, 0)),
            scratch_shapes=[
                pltpu.VMEM((CLASSES, ROWS, PIX), jnp.float32),
                pltpu.VMEM((128, ROWS, 128), jnp.bfloat16),
                pltpu.VMEM((ROWS, 256), jnp.bfloat16),
            ],
        ),
        compiler_params=pltpu.CompilerParams(
            dimension_semantics=("arbitrary",), vmem_limit_bytes=48 << 20
        ),
        name="partial_sums",
    )(code, images, ids, w1, byr, byc)


def band_filter():
    freq = (np.arange(BAND) - BAND // 2).astype(np.float64) ** 2
    return np.exp(-(freq[:, None] + freq[None, :]) / (BAND * BAND / 2.0)).astype(np.float32)


def selection_tables():
    ysel, xc, xs = selections()
    spot = np.zeros((8, 128))
    spot[1, 0] = 1.0
    spot[2, 64] = 1.0
    tables = np.concatenate([ysel, xc, xs, spot], axis=0)
    return jnp.asarray(tables.astype(np.float32), jnp.bfloat16)


ORDERS = ((0, 1, 2), (1, 2, 0), (2, 0, 1))
CHUNK = 384
HALF = 192
MESH_ID = pl.DeviceIdType.MESH


def reduce_kernel(
    part_ref,
    sel_ref,
    filt_ref,
    avg_ref,
    refs_ref,
    energy_ref,
    mine,
    rx0,
    p0,
    relay,
    near,
    p1,
    rx2,
    p2,
    rx3,
    total,
    s_send,
    s_rx,
    local_sem,
    send0,
    recv0,
    send1,
    recv1,
    send2,
    recv2,
    send3,
    recv3,
    send4,
    recv4,
):
    dp = lax.axis_index("dp")
    grp = lax.axis_index("grp")
    core = grp % 2
    here = (dp // 8, (grp // 2) * 2 + (dp // 4) % 2, dp % 4)

    def device(spot, on_core):
        x, y, z = spot
        return {"dp": (x * 2 + y % 2) * 4 + z, "grp": (y // 2) * 2 + on_core}

    def along(dim, step):
        spot = list(here)
        spot[dim] = (spot[dim] + step) % 4
        return device(spot, core)

    partner = {"dp": dp, "grp": grp + 1 - 2 * core}

    def grp_peer(r):
        low = (grp % 2 + r % 2) % 2
        high = (grp // 2 + r // 2) % 2
        return {"dp": dp, "grp": high * 2 + low}

    locals_ = []
    for color in range(3):
        copy = pltpu.make_async_copy(
            part_ref.at[core, color], mine.at[color], local_sem.at[color]
        )
        copy.start()
        locals_.append(copy)

    barrier = pltpu.get_barrier_semaphore()
    peers = [partner, grp_peer(3)] + [along(d, s) for d in range(3) for s in (1, 2, 3)]
    for peer in peers:
        pl.semaphore_signal(barrier, inc=1, device_id=peer, device_id_type=MESH_ID)
    pl.semaphore_wait(barrier, len(peers))

    started = []

    def send(src, dst, ssem, rsem, where):
        copy = pltpu.make_async_remote_copy(
            src_ref=src,
            dst_ref=dst,
            send_sem=ssem,
            recv_sem=rsem,
            device_id=where,
            device_id_type=MESH_ID,
        )
        copy.start()
        started.append(copy)
        return copy

    def chunk_at(color, step):
        return pl.multiple_of(((here[ORDERS[color][0]] + step) % 4) * CHUNK, CHUNK)

    first = {}
    for step in (2, 1, 3, 0):
        for color in range(3):
            at = chunk_at(color, step)
            first[color, step] = send(
                part_ref.at[1 - core, color, pl.ds(at, CHUNK)],
                rx0.at[color, pl.ds(at, CHUNK)],
                send0.at[color, step],
                recv0.at[color, step],
                partner,
            )

    for copy in locals_:
        copy.wait()

    def f32(value):
        return value.astype(jnp.float32)

    def add_first(color, step):
        first[color, step].wait_recv()
        at = chunk_at(color, step)
        for k in range(0, CHUNK, 128):
            rows = pl.ds(at + k, 128)
            p0[color, rows, :] = (f32(mine[color, rows, :]) + f32(rx0[color, rows, :])).astype(
                jnp.bfloat16
            )

    relays, nears = {}, {}
    for color in range(3):
        add_first(color, 2)
        at = chunk_at(color, 2)
        dim = ORDERS[color][0]
        for way, step in enumerate((1, 3)):
            relays[color, way] = send(
                p0.at[color, pl.ds(at + HALF * way, HALF)],
                relay.at[color, way],
                send1.at[color, way],
                recv1.at[color, way],
                along(dim, step),
            )
    for way, step in enumerate((1, 3)):
        for color in range(3):
            add_first(color, step)
            at = chunk_at(color, step)
            half = 1 - way
            nears[color, way, half] = send(
                p0.at[color, pl.ds(at + HALF * half, HALF)],
                near.at[color, way, pl.ds(HALF * half, HALF)],
                send1.at[color, 2 + way],
                recv1.at[color, 2 + way],
                along(ORDERS[color][0], step),
            )
    for color in range(3):
        for way, step in enumerate((1, 3)):
            relays[color, way].wait_recv()
            at = chunk_at(color, step) + HALF * way
            for k in range(0, HALF, 96):
                rows = pl.ds(at + k, 96)
                p0[color, rows, :] = (
                    f32(p0[color, rows, :]) + f32(relay[color, way, k : k + 96, :])
                ).astype(jnp.bfloat16)
            nears[color, way, way] = send(
                p0.at[color, pl.ds(at, HALF)],
                near.at[color, way, pl.ds(HALF * way, HALF)],
                send1.at[color, 4 + way],
                recv1.at[color, 4 + way],
                along(ORDERS[color][0], step),
            )
    for color in range(3):
        first[color, 0].wait_recv()

    second = {}
    for color in range(3):
        for way in range(2):
            for half in range(2):
                nears[color, way, half].wait_recv()
        at = chunk_at(color, 0)
        for k in range(0, CHUNK, 96):
            rows = pl.ds(at + k, 96)
            value = f32(mine[color, rows, :]) + f32(rx0[color, rows, :])
            value += f32(near[color, 0, k : k + 96, :]) + f32(near[color, 1, k : k + 96, :])
            p1[color, k : k + 96, :] = value.astype(jnp.bfloat16)
        dim = ORDERS[color][1]
        for step in (2, 1, 3):
            at = pl.multiple_of(((here[dim] + step) % 4) * 96, 96)
            second[color, step] = send(
                p1.at[color, pl.ds(at, 96)],
                rx2.at[color, step - 1],
                send2.at[color, step - 1],
                recv2.at[color, step - 1],
                along(dim, step),
            )
    third = {}
    for color in range(3):
        dim = ORDERS[color][1]
        value = f32(p1[color, pl.ds(pl.multiple_of(here[dim] * 96, 96), 96), :])
        for step in (1, 2, 3):
            second[color, step].wait_recv()
            value += f32(rx2[color, step - 1])
        for t in range(4):
            p2[color, t] = value[24 * t : 24 * t + 24].astype(jnp.bfloat16)
        dim = ORDERS[color][2]
        for step in (2, 1, 3):
            third[color, step] = send(
                p2.at[color, (here[dim] + step) % 4],
                rx3.at[color, step - 1],
                send3.at[color, step - 1],
                recv3.at[color, step - 1],
                along(dim, step),
            )
    for color in range(3):
        value = f32(p2[color, here[ORDERS[color][2]]])
        for step in (1, 2, 3):
            third[color, step].wait_recv()
            value += f32(rx3[color, step - 1])
        total[24 * color : 24 * color + 24, :] = value
    s_send[...] = total[...].astype(jnp.bfloat16)
    fourth = {}
    for r in (3, 2, 1):
        fourth[r] = send(
            s_send, s_rx.at[r - 1], send4.at[r - 1], recv4.at[r - 1], grp_peer(r)
        )

    ysel = sel_ref[0:128, :]
    xsel = (sel_ref[128:256, :], sel_ref[256:384, :])
    spot = sel_ref[384:392, :]
    lane = lax.broadcasted_iota(jnp.int32, (1, 128), 1)
    weight = jnp.where(
        (lane >= 65) & (lane < 77), 1 << jnp.clip(lane - 65, 0, 12), 0
    ).astype(jnp.float32)

    def dot(a, b, dims=(((1,), (0,)), ((), ()))):
        return lax.dot_general(a, b, dims, preferred_element_type=jnp.float32)

    def finish(block, g, own):
        rows = dot(ysel[:, :72], block).astype(jnp.bfloat16)
        rc, rs = dot(rows, xsel[0]), dot(rows, xsel[1])
        side = dot(ysel, block[64:72], (((1,), (1,)), ((), ()))).astype(jnp.bfloat16)
        side = dot(side, spot)
        real = rc[:64] - rs[64:] + side[64:]
        imag = side[:64] - rc[64:] - rs[:64]
        tally = f32(block[64:72]) * weight
        members = jnp.sum(tally, axis=1, keepdims=True)
        scale = filt_ref[...] / (jnp.where(lane < 64, members[1:2], members[2:3]) + ridge)
        real, imag = real * scale, imag * scale
        if own:
            avg_ref[0] = real
            avg_ref[1] = imag
        real, imag = real.astype(jnp.bfloat16), imag.astype(jnp.bfloat16)
        refs_ref[g, 0] = real
        refs_ref[g, 1] = imag
        power = jnp.sum(f32(real) * f32(real) + f32(imag) * f32(imag), axis=0, keepdims=True)
        for j in range(2):
            energy = jnp.sum(jnp.where(lane // 64 == j, power, 0.0), axis=1, keepdims=True)
            energy_ref[g, j : j + 1, :] = jnp.broadcast_to(energy, (1, 128))

    finish(s_send[...], grp, True)
    for r in (1, 2, 3):
        fourth[r].wait_recv()
        finish(s_rx[r - 1], grp_peer(r)["grp"], False)
    for copy in started:
        copy.wait_send()


def reduce_classes(partial):
    sel = selection_tables()
    filt = jnp.asarray(np.tile(band_filter(), (1, 2)))
    vmem = pl.BlockSpec(memory_space=pltpu.VMEM)
    bf16 = jnp.bfloat16
    return pl.pallas_call(
        reduce_kernel,
        out_shape=(
            jax.ShapeDtypeStruct((2, 64, 128), jnp.float32),
            jax.ShapeDtypeStruct((4, 2, 64, 128), bf16),
            jax.ShapeDtypeStruct((4, 2, 128), jnp.float32),
        ),
        in_specs=[pl.BlockSpec(memory_space=pl.ANY), vmem, vmem],
        out_specs=(vmem, vmem, vmem),
        scratch_shapes=[
            pltpu.VMEM((3, 1536, 128), bf16),
            pltpu.VMEM((3, 1536, 128), bf16),
            pltpu.VMEM((3, 1536, 128), bf16),
            pltpu.VMEM((3, 2, HALF, 128), bf16),
            pltpu.VMEM((3, 2, CHUNK, 128), bf16),
            pltpu.VMEM((3, CHUNK, 128), bf16),
            pltpu.VMEM((3, 3, 96, 128), bf16),
            pltpu.VMEM((3, 4, 24, 128), bf16),
            pltpu.VMEM((3, 3, 24, 128), bf16),
            pltpu.VMEM((72, 128), jnp.float32),
            pltpu.VMEM((72, 128), bf16),
            pltpu.VMEM((3, 72, 128), bf16),
            pltpu.SemaphoreType.DMA((3,)),
            pltpu.SemaphoreType.DMA((3, 4)),
            pltpu.SemaphoreType.DMA((3, 4)),
            pltpu.SemaphoreType.DMA((3, 6)),
            pltpu.SemaphoreType.DMA((3, 6)),
            pltpu.SemaphoreType.DMA((3, 3)),
            pltpu.SemaphoreType.DMA((3, 3)),
            pltpu.SemaphoreType.DMA((3, 3)),
            pltpu.SemaphoreType.DMA((3, 3)),
            pltpu.SemaphoreType.DMA((3,)),
            pltpu.SemaphoreType.DMA((3,)),
        ],
        compiler_params=pltpu.CompilerParams(
            collective_id=0, has_side_effects=True, vmem_limit_bytes=24 << 20
        ),
        name="reduce_classes",
    )(partial.reshape(2, 3, 1536, 128), sel, filt)


def body(images, shifts, class_ids, next_block):
    code = (class_ids * 64 + shifts[:, 1] + REACH) * 128 + (shifts[:, 0] & (PIX - 1))
    partial = partial_sums(images, code, class_ids[None, :])
    mine, refs, energy = reduce_classes(partial)
    averages = mine.reshape(2, 64, 2, 64).transpose(2, 0, 1, 3).reshape(2, 2, BAND * BAND)
    refs = refs.reshape(4, 2, 64, 2, 64).transpose(0, 3, 1, 2, 4).reshape(8, 2 * BAND * BAND)
    next_flat = next_block.reshape(next_block.shape[0], 2 * BAND * BAND)
    inner_prod = lax.dot_general(
        refs, next_flat, (((1,), (1,)), ((), ())), preferred_element_type=jnp.float32
    )
    scores = (inner_prod - 0.5 * energy[:, :, :1].reshape(8, 1)) / BAND
    return (averages, scores)


def solution(mesh):
    placed = (
        P(("dp", "grp"), None, None),
        P(("dp", "grp"), None),
        P(("dp", "grp")),
        P("grp", None, None),
    )
    return jax.shard_map(
        body,
        mesh=mesh,
        in_specs=placed,
        out_specs=(P(("dp", "grp"), None, None), P("dp", "grp")),
        check_vma=False,
    )
```

```python
import math

import jax
import jax.numpy as jnp
from jax import lax
from jax.experimental import pallas as pl
from jax.experimental.pallas import tpu as pltpu
from jax.sharding import PartitionSpec as P

PIX = 128
BAND = 64
CLASSES = 256
REACH = 16
ROWS = PIX + 2 * REACH
OUT_ROWS = 72
STEP = 32
BATCH = 8
ridge = 4.0


def iota(shape, axis):
    return lax.broadcasted_iota(jnp.int32, shape, axis)


def wave(position, b):
    is_sin = ((b >= 32) & (b < 63)) | (b == 64)
    freq = jnp.where(b < 32, b, jnp.where(b < 63, b - 31, 32))
    residue = (position * freq - jnp.where(is_sin, 32, 0)) & (PIX - 1)
    value = jnp.cos(residue.astype(jnp.float32) * (2.0 * math.pi / PIX))
    return jnp.where(b <= 64, value * (1.0 / math.sqrt(PIX)), 0.0)


def partial_kernel(meta_ref, metav_ref, img_hbm, out_ref, acc, x2, edge, imgs, w1, img_sem):
    count = imgs.shape[0]

    def chunk(k):
        at = pl.ds(k * STEP, STEP)
        return pltpu.make_async_copy(img_hbm.at[at], imgs.at[at], img_sem.at[k])

    for k in range(count // STEP):
        chunk(k).start()
    flat = wave(iota((PIX, 128), 0), iota((PIX, 128), 1))
    byr = wave(iota((OUT_ROWS, PIX), 1), iota((OUT_ROWS, PIX), 0)).astype(jnp.bfloat16)
    byc = flat.astype(jnp.bfloat16)
    lane = iota((PIX, 128), 1)
    low = jnp.where(lane < 64, flat, 0.0)
    last = wave(iota((PIX, 128), 0), jnp.full((PIX, 128), 64, jnp.int32))
    for j in range(2):
        w1[PIX * j : PIX * j + PIX, 0:128] = pltpu.roll(low, 64 * j, 1).astype(jnp.bfloat16)
        w1[PIX * j : PIX * j + PIX, 128:256] = jnp.where(lane % 2 == j, last, 0.0).astype(
            jnp.bfloat16
        )

    def clear(c, carry):
        acc[c] = jnp.zeros((ROWS, PIX), jnp.float32)
        return carry

    lax.fori_loop(0, CLASSES, clear, 0, unroll=2)

    def add_chunk(k, carry):
        chunk(k).wait()

        def add_image(n, inner):
            i = k * STEP + n
            row = meta_ref[1, i] + REACH
            moved = pltpu.roll(imgs[i].astype(jnp.float32), meta_ref[0, i] & (PIX - 1), 1)
            acc[meta_ref[2, i], pl.ds(row, PIX), :] += moved
            return inner

        return lax.fori_loop(0, STEP, add_image, carry, unroll=16)

    lax.fori_loop(0, count // STEP, add_chunk, 0)
    lane_pair = iota((PIX, 128), 1) // 2

    def folded(c):
        return jnp.concatenate(
            [
                acc[c, 16:32, :] + acc[c, 144:160, :],
                acc[c, 32:128, :],
                acc[c, 128:144, :] + acc[c, 0:16, :],
            ],
            axis=0,
        ).astype(jnp.bfloat16)

    for half in range(2):

        def columns(p, carry):
            pair = half * 64 + p * BATCH
            lhs = jnp.concatenate(
                [
                    jnp.concatenate([folded(2 * (pair + k)), folded(2 * (pair + k) + 1)], axis=1)
                    for k in range(BATCH)
                ],
                axis=0,
            )
            got = jnp.dot(lhs, w1[...], preferred_element_type=jnp.float32)
            for k in range(BATCH):
                mine = got[PIX * k : PIX * k + PIX]
                x2[pair + k] = mine[:, :128].astype(jnp.bfloat16)
                pltpu.store(
                    edge.at[:, half * 128 : half * 128 + 128],
                    mine[:, 128:],
                    mask=lane_pair == p * BATCH + k,
                )
            return carry

        lax.fori_loop(0, 64 // BATCH, columns, 0)
    side = lax.dot_general(
        edge[...].astype(jnp.bfloat16),
        byc,
        (((0,), (0,)), ((), ())),
        preferred_element_type=jnp.float32,
    )
    tally = jnp.sum(
        jnp.where(
            iota((CLASSES, count), 0) == metav_ref[2:3, :], 1.0, 0.0
        ),
        axis=1,
        keepdims=True,
    ).astype(jnp.int32)
    lane = iota((CLASSES, 128), 1)
    bit = lane - 65
    tally = jnp.where(
        (bit >= 0) & (bit < 12), (tally >> jnp.clip(bit, 0, 12)) & 1, 0
    ).astype(jnp.float32)
    acc[0, 0:128, :] = side[:128] + tally[:128]
    acc[1, 0:128, :] = side[128:] + tally[128:]

    def rows(q2, carry):
        eight = acc[q2 // 16, pl.ds(pl.multiple_of((q2 % 16) * 8, 8), 8), :]
        sub = iota((8, 128), 0)
        place = (sub == 1) | (sub == 2)
        for k in range(2):
            q = q2 * 2 + k
            rhs = jnp.concatenate([x2[2 * q], x2[2 * q + 1]], axis=1)
            got = jnp.dot(byr, rhs, preferred_element_type=jnp.float32)
            for core in range(2):
                part = got[:, 128 * core : 128 * core + 128]
                at = 4 * k + 2 * core
                extra = jnp.where(place, pltpu.roll(eight, (1 - at) % 8, 0), 0.0)
                whole = jnp.concatenate([part[:64], part[64:] + extra], axis=0)
                x, y, z = q // 16, (q % 2) * 2 + (q // 8) % 2, (q // 2) % 4
                spots = (x * 16 + y * 4 + z, y * 16 + z * 4 + x, z * 16 + x * 4 + y)
                for color in range(3):
                    out_ref[core, color, spots[color]] = whole[
                        24 * color : 24 * color + 24
                    ].astype(jnp.bfloat16)
        return carry

    lax.fori_loop(0, 32, rows, 0, unroll=4)


def partial_sums(images, meta):
    count = images.shape[0]
    bf16 = jnp.bfloat16
    return pl.pallas_call(
        partial_kernel,
        out_shape=jax.ShapeDtypeStruct((2, 3, 64, 24, 128), bf16),
        in_specs=[
            pl.BlockSpec(memory_space=pltpu.SMEM),
            pl.BlockSpec(memory_space=pltpu.VMEM),
            pl.BlockSpec(memory_space=pl.ANY),
        ],
        out_specs=pl.BlockSpec(memory_space=pltpu.VMEM),
        scratch_shapes=[
            pltpu.VMEM((CLASSES, ROWS, PIX), jnp.float32),
            pltpu.VMEM((128, PIX, 128), bf16),
            pltpu.VMEM((PIX, 256), jnp.float32),
            pltpu.VMEM(images.shape, bf16),
            pltpu.VMEM((2 * PIX, 256), bf16),
            pltpu.SemaphoreType.DMA((count // STEP,)),
        ],
        compiler_params=pltpu.CompilerParams(vmem_limit_bytes=48 << 20),
        name="partial_sums",
    )(meta, meta, images)


ORDERS = ((0, 1, 2), (1, 2, 0), (2, 0, 1))
CHUNK = 384
HALF = 192
MESH_ID = pl.DeviceIdType.MESH


def reduce_kernel(
    part_ref,
    next_ref,
    avg_ref,
    score_ref,
    nexts,
    rx0,
    p0,
    relay,
    near,
    p1,
    rx2,
    p2,
    rx3,
    s_all,
    final,
    gathered,
    products,
    next_sem,
    send0,
    recv0,
    send1,
    recv1,
    send2,
    recv2,
    send3,
    recv3,
    send4,
    recv4,
):
    dp = lax.axis_index("dp")
    grp = lax.axis_index("grp")
    core = grp % 2
    here = (dp // 8, (grp // 2) * 2 + (dp // 4) % 2, dp % 4)

    def device(spot, on_core):
        x, y, z = spot
        return {"dp": (x * 2 + y % 2) * 4 + z, "grp": (y // 2) * 2 + on_core}

    def along(dim, step):
        spot = list(here)
        spot[dim] = (spot[dim] + step) % 4
        return device(spot, core)

    partner = {"dp": dp, "grp": grp + 1 - 2 * core}

    def grp_peer(r):
        low = (grp % 2 + r % 2) % 2
        high = (grp // 2 + r // 2) % 2
        return {"dp": dp, "grp": high * 2 + low}

    columns = [
        pltpu.make_async_copy(
            next_ref.at[:, :, pl.ds(128 * t, 128)], nexts.at[t], next_sem.at[t]
        )
        for t in range(32)
    ]
    barrier = pltpu.get_barrier_semaphore()
    peers = [partner, grp_peer(3)] + [along(d, s) for d in range(3) for s in (1, 2, 3)]
    for peer in peers:
        pl.semaphore_signal(barrier, inc=1, device_id=peer, device_id_type=MESH_ID)
    pl.semaphore_wait(barrier, len(peers))

    started = []

    def send(src, dst, ssem, rsem, where):
        copy = pltpu.make_async_remote_copy(
            src_ref=src,
            dst_ref=dst,
            send_sem=ssem,
            recv_sem=rsem,
            device_id=where,
            device_id_type=MESH_ID,
        )
        copy.start()
        started.append(copy)
        return copy

    def chunk_at(color, step):
        return pl.multiple_of(((here[ORDERS[color][0]] + step) % 4) * CHUNK, CHUNK)

    first = {}
    for step in (2, 1, 3, 0):
        for color in range(3):
            at = chunk_at(color, step)
            first[color, step] = send(
                part_ref.at[1 - core, color, pl.ds(at, CHUNK)],
                rx0.at[color, pl.ds(at, CHUNK)],
                send0.at[color, step],
                recv0.at[color, step],
                partner,
            )

    for copy in columns:
        copy.start()

    def f32(value):
        return value.astype(jnp.float32)

    def add_first(color, step):
        first[color, step].wait_recv()
        at = chunk_at(color, step)
        for k in range(0, CHUNK, 128):
            rows = pl.ds(at + k, 128)
            p0[color, rows, :] = (f32(part_ref[core, color, rows, :]) + f32(rx0[color, rows, :])).astype(
                jnp.bfloat16
            )

    relays, nears = {}, {}
    for color in range(3):
        add_first(color, 2)
        at = chunk_at(color, 2)
        dim = ORDERS[color][0]
        for way, step in enumerate((1, 3)):
            relays[color, way] = send(
                p0.at[color, pl.ds(at + HALF * way, HALF)],
                relay.at[color, way],
                send1.at[color, way],
                recv1.at[color, way],
                along(dim, step),
            )
    for way, step in enumerate((1, 3)):
        for color in range(3):
            add_first(color, step)
            at = chunk_at(color, step)
            half = 1 - way
            nears[color, way, half] = send(
                p0.at[color, pl.ds(at + HALF * half, HALF)],
                near.at[color, way, pl.ds(HALF * half, HALF)],
                send1.at[color, 2 + way],
                recv1.at[color, 2 + way],
                along(ORDERS[color][0], step),
            )
    for color in range(3):
        for way, step in enumerate((1, 3)):
            relays[color, way].wait_recv()
            at = chunk_at(color, step) + HALF * way
            for k in range(0, HALF, 96):
                rows = pl.ds(at + k, 96)
                p0[color, rows, :] = (
                    f32(p0[color, rows, :]) + f32(relay[color, way, k : k + 96, :])
                ).astype(jnp.bfloat16)
            nears[color, way, way] = send(
                p0.at[color, pl.ds(at, HALF)],
                near.at[color, way, pl.ds(HALF * way, HALF)],
                send1.at[color, 4 + way],
                recv1.at[color, 4 + way],
                along(ORDERS[color][0], step),
            )
    for color in range(3):
        first[color, 0].wait_recv()

    second = {}
    for color in range(3):
        for way in range(2):
            for half in range(2):
                nears[color, way, half].wait_recv()
        at = chunk_at(color, 0)
        for k in range(0, CHUNK, 96):
            rows = pl.ds(at + k, 96)
            value = f32(part_ref[core, color, rows, :]) + f32(rx0[color, rows, :])
            value += f32(near[color, 0, k : k + 96, :]) + f32(near[color, 1, k : k + 96, :])
            p1[color, k : k + 96, :] = value.astype(jnp.bfloat16)
        dim = ORDERS[color][1]
        for step in (2, 1, 3):
            at = pl.multiple_of(((here[dim] + step) % 4) * 96, 96)
            second[color, step] = send(
                p1.at[color, pl.ds(at, 96)],
                rx2.at[color, step - 1],
                send2.at[color, step - 1],
                recv2.at[color, step - 1],
                along(dim, step),
            )
    third = {}
    for color in range(3):
        dim = ORDERS[color][1]
        value = f32(p1[color, pl.ds(pl.multiple_of(here[dim] * 96, 96), 96), :])
        for step in (1, 2, 3):
            second[color, step].wait_recv()
            value += f32(rx2[color, step - 1])
        for t in range(4):
            p2[color, t] = value[24 * t : 24 * t + 24].astype(jnp.bfloat16)
        dim = ORDERS[color][2]
        for step in (2, 1, 3):
            third[color, step] = send(
                p2.at[color, (here[dim] + step) % 4],
                rx3.at[color, step - 1],
                send3.at[color, step - 1],
                recv3.at[color, step - 1],
                along(dim, step),
            )
    parts = []
    for color in range(3):
        value = f32(p2[color, here[ORDERS[color][2]]])
        for step in (1, 2, 3):
            third[color, step].wait_recv()
            value += f32(rx3[color, step - 1])
        parts.append(value)
    s_all[grp] = jnp.concatenate(parts, axis=0).astype(jnp.bfloat16)
    fourth = {}
    for r in (3, 2, 1):
        fourth[r] = send(
            s_all.at[grp], s_all.at[grp], send4.at[r - 1], recv4.at[r - 1], grp_peer(r)
        )

    def dot(a, b, dims=(((1,), (0,)), ((), ()))):
        return lax.dot_general(a, b, dims, preferred_element_type=jnp.float32)

    def matches(shape, row_of, lane_of):
        return jnp.where(row_of(iota(shape, 0)) == lane_of(iota(shape, 1)), 1.0, 0.0)

    def cos_at(k):
        size = jnp.abs(k - 32)
        return jnp.where(size == 32, 63, size)

    def sin_at(k):
        size = jnp.abs(k - 32)
        return jnp.where(size == 0, -1, jnp.where(size == 32, 64, size + 31))

    row = iota((128, 128), 0)
    lane = iota((128, 128), 1)
    ky = 2 * (row & 31) + ((row >> 5) & 1)
    ysel = jnp.where(
        row < 64,
        jnp.where(cos_at(ky) == lane, 1.0, 0.0),
        jnp.where(sin_at(ky) == lane, jnp.where(ky < 32, -1.0, 1.0), 0.0),
    ).astype(jnp.bfloat16)
    kx = lane & 63
    same = (row >> 6) == (lane >> 6)
    xc = jnp.where(same & (cos_at(kx) == (row & 63)), 1.0, 0.0)
    xs = jnp.where(same & (sin_at(kx) == (row & 63)), jnp.where(kx < 32, -1.0, 1.0), 0.0)
    xsel = jnp.concatenate([xc, xs], axis=1).astype(jnp.bfloat16)
    srow, slane = iota((32, 512), 0), iota((32, 512), 1)
    at = (srow & 7) - 1
    spot = jnp.where(
        ((srow >> 3) == (slane >> 7)) & (at >= 0) & (at < 2) & ((slane & 127) == at * 64), 1.0, 0.0
    ).astype(jnp.bfloat16)
    frow, flane = iota((32, 128), 0), iota((32, 128), 1)
    fy = f32(2 * frow + (flane >> 6) - 32)
    fx = f32((flane & 63) - 32)
    filt = jnp.exp(-(fy * fy + fx * fx) / (BAND * BAND / 2.0))
    bits = iota((8, 128), 1) - 65
    weight = jnp.where((bits >= 0) & (bits < 12), f32(1 << jnp.clip(bits, 0, 12)), 0.0)

    for r in (1, 2, 3):
        fourth[r].wait_recv()
    blocks = [s_all[g] for g in range(4)]
    y = dot(ysel[:, :72], jnp.concatenate(blocks, axis=1)).astype(jnp.bfloat16)
    y = jnp.concatenate([y[:, 128 * g : 128 * g + 128] for g in range(4)], axis=0)
    z = dot(y, xsel)
    extra = jnp.concatenate([b[64:72] for b in blocks], axis=0)
    side = dot(ysel, extra, (((1,), (1,)), ((), ()))).astype(jnp.bfloat16)
    side = dot(side, spot)
    half = iota((32, 128), 1) < 64
    for g in range(4):
        rc = z[128 * g : 128 * g + 128, :128]
        rs = z[128 * g : 128 * g + 128, 128:]
        sg = side[:, 128 * g : 128 * g + 128]
        members = jnp.sum(f32(blocks[g][64:72]) * weight, axis=1, keepdims=True)
        planes = (rc[:64] - rs[64:] + sg[64:], sg[:64] - rc[64:] - rs[:64])
        for j in range(2):
            scale = filt / (members[1 + j : 2 + j] + ridge)
            for p in range(2):
                even, odd = planes[p][:32], planes[p][32:]
                if j == 0:
                    odd = pltpu.roll(odd, 64, 1)
                else:
                    even = pltpu.roll(even, 64, 1)
                value = jnp.where(half, even, odd) * scale
                final[g, j, p] = value
                gathered[pl.ds(256 * p + 2 * g + j, 32, stride=8), :] = f32(
                    value.astype(jnp.bfloat16)
                )
    avg_ref[...] = final[grp]

    for copy in columns:
        copy.wait()
    blocks_of = nexts.reshape(32, 512, 128)
    energy = jnp.zeros((8, 128), jnp.float32)
    inner = jnp.zeros((512, 16), jnp.float32)
    for t in range(0, 32, 2):
        sides = []
        for u in (t, t + 1):
            re = gathered[8 * u : 8 * u + 8, :]
            im = gathered[256 + 8 * u : 264 + 8 * u, :]
            energy += re * re + im * im
            sides.append(jnp.concatenate([re, im], axis=0).astype(jnp.bfloat16))
        inner += dot(
            jnp.concatenate([blocks_of[t], blocks_of[t + 1]], axis=1),
            jnp.concatenate(sides, axis=1),
            (((1,), (1,)), ((), ())),
        )
    products[:, 0:16] = inner
    both = products[pl.ds(0, 256, stride=2), :] + pltpu.roll(
        products[pl.ds(1, 256, stride=2), :], 120, 1
    )
    energy = jnp.sum(energy, axis=1, keepdims=True)
    score_ref[...] = (both.T[:8] - 0.5 * energy) / BAND
    for copy in started:
        copy.wait_send()


def reduce_classes(partial, next_block):
    vmem = pl.BlockSpec(memory_space=pltpu.VMEM)
    bf16 = jnp.bfloat16
    return pl.pallas_call(
        reduce_kernel,
        out_shape=(
            jax.ShapeDtypeStruct((2, 2, 32, 128), jnp.float32),
            jax.ShapeDtypeStruct((8, 256), jnp.float32),
        ),
        in_specs=[vmem, pl.BlockSpec(memory_space=pl.ANY)],
        out_specs=(vmem, vmem),
        scratch_shapes=[
            pltpu.VMEM((32, 256, 2, 128), bf16),
            pltpu.VMEM((3, 1536, 128), bf16),
            pltpu.VMEM((3, 1536, 128), bf16),
            pltpu.VMEM((3, 2, HALF, 128), bf16),
            pltpu.VMEM((3, 2, CHUNK, 128), bf16),
            pltpu.VMEM((3, CHUNK, 128), bf16),
            pltpu.VMEM((3, 3, 96, 128), bf16),
            pltpu.VMEM((3, 4, 24, 128), bf16),
            pltpu.VMEM((3, 3, 24, 128), bf16),
            pltpu.VMEM((4, 72, 128), bf16),
            pltpu.VMEM((4, 2, 2, 32, 128), jnp.float32),
            pltpu.VMEM((512, 128), jnp.float32),
            pltpu.VMEM((512, 128), jnp.float32),
            pltpu.SemaphoreType.DMA((32,)),
            pltpu.SemaphoreType.DMA((3, 4)),
            pltpu.SemaphoreType.DMA((3, 4)),
            pltpu.SemaphoreType.DMA((3, 6)),
            pltpu.SemaphoreType.DMA((3, 6)),
            pltpu.SemaphoreType.DMA((3, 3)),
            pltpu.SemaphoreType.DMA((3, 3)),
            pltpu.SemaphoreType.DMA((3, 3)),
            pltpu.SemaphoreType.DMA((3, 3)),
            pltpu.SemaphoreType.DMA((3,)),
            pltpu.SemaphoreType.DMA((3,)),
        ],
        compiler_params=pltpu.CompilerParams(
            collective_id=0, has_side_effects=True, vmem_limit_bytes=24 << 20
        ),
        name="reduce_classes",
    )(partial.reshape(2, 3, 1536, 128), next_block)


def body(images, shifts, class_ids, next_block):
    meta = jnp.concatenate([shifts.T, class_ids[None, :]], axis=0)
    averages, scores = reduce_classes(partial_sums(images, meta), next_block)
    return (averages.reshape(2, 2, BAND * BAND), scores)


def solution(mesh):
    placed = (
        P(("dp", "grp"), None, None),
        P(("dp", "grp"), None),
        P(("dp", "grp")),
        P("grp", None, None),
    )
    return jax.shard_map(
        body,
        mesh=mesh,
        in_specs=placed,
        out_specs=(P(("dp", "grp"), None, None), P("dp", "grp")),
        check_vma=False,
    )
```

```python
import math

import jax
import jax.numpy as jnp
from jax import lax
from jax.experimental import pallas as pl
from jax.experimental.pallas import tpu as pltpu
from jax.sharding import PartitionSpec as P

PIX = 128
BAND = 64
CLASSES = 256
REACH = 16
ROWS = PIX + 2 * REACH
OUT_ROWS = 72
STEP = 32
BATCH = 8
ridge = 4.0


def iota(shape, axis):
    return lax.broadcasted_iota(jnp.int32, shape, axis)


def wave(position, b):
    is_sin = ((b >= 32) & (b < 63)) | (b == 64)
    freq = jnp.where(b < 32, b, jnp.where(b < 63, b - 31, 32))
    residue = (position * freq - jnp.where(is_sin, 32, 0)) & (PIX - 1)
    value = jnp.cos(residue.astype(jnp.float32) * (2.0 * math.pi / PIX))
    return jnp.where(b <= 64, value * (1.0 / math.sqrt(PIX)), 0.0)


def class_kernel(meta_ref, img_hbm, acc, imgs, img_sem):
    count = imgs.shape[0]

    def chunk(k):
        at = pl.ds(k * STEP, STEP)
        return pltpu.make_async_copy(img_hbm.at[at], imgs.at[at], img_sem.at[k])

    for k in range(count // STEP):
        chunk(k).start()

    def clear(c, carry):
        acc[c] = jnp.zeros((ROWS, PIX), jnp.float32)
        return carry

    lax.fori_loop(0, CLASSES, clear, 0, unroll=4)

    def add_chunk(k, carry):
        chunk(k).wait()

        def add_image(n, inner):
            i = k * STEP + n
            row = meta_ref[1, i] + REACH
            moved = pltpu.roll(imgs[i].astype(jnp.float32), meta_ref[0, i] & (PIX - 1), 1)
            acc[meta_ref[2, i], pl.ds(row, PIX), :] += moved
            return inner

        return lax.fori_loop(0, STEP, add_image, carry, unroll=16)

    lax.fori_loop(0, count // STEP, add_chunk, 0)


def class_images(images, meta):
    return pl.pallas_call(
        class_kernel,
        out_shape=pltpu.VMEM((CLASSES, ROWS, PIX), jnp.float32),
        in_specs=[
            pl.BlockSpec(memory_space=pltpu.SMEM),
            pl.BlockSpec(memory_space=pl.ANY),
        ],
        out_specs=pl.BlockSpec(memory_space=pltpu.VMEM),
        scratch_shapes=[
            pltpu.VMEM(images.shape, jnp.bfloat16),
            pltpu.SemaphoreType.DMA((images.shape[0] // STEP,)),
        ],
        compiler_params=pltpu.CompilerParams(vmem_limit_bytes=20 << 20),
        name="class_images",
    )(meta, images)


ORDERS = ((0, 1, 2), (1, 2, 0), (2, 0, 1))
CHUNK = 384
HALF = 192
MESH_ID = pl.DeviceIdType.MESH


def reduce_kernel(
    acc,
    meta_ref,
    next_ref,
    avg_ref,
    score_ref,
    nexts,
    x2,
    edge,
    side_rows,
    part,
    outgoing,
    rx0,
    p0,
    relay,
    near,
    p1,
    rx2,
    p2,
    rx3,
    s_all,
    w1_ref,
    final,
    gathered,
    products,
    next_sem,
    send0,
    recv0,
    send1,
    recv1,
    send2,
    recv2,
    send3,
    recv3,
    send4,
    recv4,
):
    dp = lax.axis_index("dp")
    grp = lax.axis_index("grp")
    core = grp % 2
    here = (dp // 8, (grp // 2) * 2 + (dp // 4) % 2, dp % 4)

    def device(spot, on_core):
        x, y, z = spot
        return {"dp": (x * 2 + y % 2) * 4 + z, "grp": (y // 2) * 2 + on_core}

    def along(dim, step):
        spot = list(here)
        spot[dim] = (spot[dim] + step) % 4
        return device(spot, core)

    partner = {"dp": dp, "grp": grp + 1 - 2 * core}

    def grp_peer(r):
        low = (grp % 2 + r % 2) % 2
        high = (grp // 2 + r // 2) % 2
        return {"dp": dp, "grp": high * 2 + low}

    columns = [
        pltpu.make_async_copy(
            next_ref.at[:, :, pl.ds(128 * t, 128)], nexts.at[t], next_sem.at[t]
        )
        for t in range(32)
    ]
    barrier = pltpu.get_barrier_semaphore()
    peers = [partner, grp_peer(3)] + [along(d, s) for d in range(3) for s in (1, 2, 3)]
    for peer in peers:
        pl.semaphore_signal(barrier, inc=1, device_id=peer, device_id_type=MESH_ID)
    started = []

    def send(src, dst, ssem, rsem, where):
        copy = pltpu.make_async_remote_copy(
            src_ref=src,
            dst_ref=dst,
            send_sem=ssem,
            recv_sem=rsem,
            device_id=where,
            device_id_type=MESH_ID,
        )
        copy.start()
        started.append(copy)
        return copy

    def chunk_at(color, step):
        return pl.multiple_of(((here[ORDERS[color][0]] + step) % 4) * CHUNK, CHUNK)

    for copy in columns:
        copy.start()

    flat = wave(iota((PIX, 128), 0), iota((PIX, 128), 1))
    byr = wave(iota((OUT_ROWS, PIX), 1), iota((OUT_ROWS, PIX), 0)).astype(jnp.bfloat16)
    byc = flat.astype(jnp.bfloat16)
    lane128 = iota((PIX, 128), 1)
    low = jnp.where(lane128 < 64, flat, 0.0)
    last = wave(iota((PIX, 128), 0), jnp.full((PIX, 128), 64, jnp.int32))
    w1 = jnp.concatenate(
        [
            jnp.concatenate(
                [pltpu.roll(low, 64 * j, 1), jnp.where(lane128 % 2 == j, last, 0.0)], axis=1
            )
            for j in range(2)
        ],
        axis=0,
    ).astype(jnp.bfloat16)
    w1_ref[...] = w1
    lane_pair = lane128 // 2

    def folded(c):
        return jnp.concatenate(
            [
                acc[c, 16:32, :] + acc[c, 144:160, :],
                acc[c, 32:128, :],
                acc[c, 128:144, :] + acc[c, 0:16, :],
            ],
            axis=0,
        ).astype(jnp.bfloat16)

    def transform(on_core):
        def columns_of(p, carry):
            chip = p * BATCH
            lhs = []
            for k in range(BATCH):
                c = (chip + k) * 4 + 2 * on_core
                lhs.append(jnp.concatenate([folded(c), folded(c + 1)], axis=1))
            got = jnp.dot(
                jnp.concatenate(lhs, axis=0), w1_ref[...], preferred_element_type=jnp.float32
            )
            for k in range(BATCH):
                mine = got[PIX * k : PIX * k + PIX]
                x2[chip + k] = mine[:, :128].astype(jnp.bfloat16)
                pltpu.store(edge, mine[:, 128:], mask=lane_pair == chip + k)
            return carry

        lax.fori_loop(0, 64 // BATCH, columns_of, 0)
        side = lax.dot_general(
            edge[...].astype(jnp.bfloat16),
            byc,
            (((0,), (0,)), ((), ())),
            preferred_element_type=jnp.float32,
        )
        row = iota((128, meta_ref.shape[1]), 0)
        cls = (row // 2) * 4 + 2 * on_core + row % 2
        tally = jnp.sum(
            jnp.where(cls == meta_ref[2:3, :], 1.0, 0.0), axis=1, keepdims=True
        ).astype(jnp.int32)
        bit = lane128 - 65
        tally = jnp.where((bit >= 0) & (bit < 12), (tally >> jnp.clip(bit, 0, 12)) & 1, 0)
        side_rows[...] = side + tally.astype(jnp.float32)

        def rows_of(m, carry):
            eight = side_rows[pl.ds(pl.multiple_of(m * 8, 8), 8), :]
            sub = iota((8, 128), 0)
            place = (sub == 1) | (sub == 2)
            for k in range(0, 4, 2):
                q = m * 4 + k
                got = jnp.dot(
                    byr,
                    jnp.concatenate([x2[q], x2[q + 1]], axis=1),
                    preferred_element_type=jnp.float32,
                )
                for n in range(2):
                    q = m * 4 + k + n
                    block = got[:, 128 * n : 128 * n + 128]
                    extra = jnp.where(place, pltpu.roll(eight, (1 - 2 * (k + n)) % 8, 0), 0.0)
                    block = jnp.concatenate([block[:64], block[64:] + extra], axis=0)
                    x, y, z = q // 16, (q % 2) * 2 + (q // 8) % 2, (q // 2) % 4
                    spots = (x * 16 + y * 4 + z, y * 16 + z * 4 + x, z * 16 + x * 4 + y)
                    for color in range(3):
                        at = pl.multiple_of(spots[color] * 24, 8)
                        part[color, pl.ds(at, 24), :] = block[24 * color : 24 * color + 24]
            return carry

        lax.fori_loop(0, 16, rows_of, 0, unroll=2)

    transform(1 - core)
    first = {}
    for step in (2, 1, 3, 0):
        for color in range(3):
            at = chunk_at(color, step)
            for k in range(0, CHUNK, 128):
                rows = pl.ds(at + k, 128)
                outgoing[color, rows, :] = part[color, rows, :].astype(jnp.bfloat16)
    pl.semaphore_wait(barrier, len(peers))
    for step in (2, 1, 3, 0):
        for color in range(3):
            at = chunk_at(color, step)
            first[color, step] = send(
                outgoing.at[color, pl.ds(at, CHUNK)],
                rx0.at[color, pl.ds(at, CHUNK)],
                send0.at[color, step],
                recv0.at[color, step],
                partner,
            )
    transform(core)

    def f32(value):
        return value.astype(jnp.float32)

    def add_first(color, step):
        first[color, step].wait_recv()
        at = chunk_at(color, step)
        for k in range(0, CHUNK, 128):
            rows = pl.ds(at + k, 128)
            p0[color, rows, :] = (part[color, rows, :] + f32(rx0[color, rows, :])).astype(
                jnp.bfloat16
            )

    relays, nears = {}, {}
    for color in range(3):
        add_first(color, 2)
        at = chunk_at(color, 2)
        dim = ORDERS[color][0]
        for way, step in enumerate((1, 3)):
            relays[color, way] = send(
                p0.at[color, pl.ds(at + HALF * way, HALF)],
                relay.at[color, way],
                send1.at[color, way],
                recv1.at[color, way],
                along(dim, step),
            )
    for way, step in enumerate((1, 3)):
        for color in range(3):
            add_first(color, step)
            at = chunk_at(color, step)
            half = 1 - way
            nears[color, way, half] = send(
                p0.at[color, pl.ds(at + HALF * half, HALF)],
                near.at[color, way, pl.ds(HALF * half, HALF)],
                send1.at[color, 2 + way],
                recv1.at[color, 2 + way],
                along(ORDERS[color][0], step),
            )
    for color in range(3):
        for way, step in enumerate((1, 3)):
            relays[color, way].wait_recv()
            at = chunk_at(color, step) + HALF * way
            for k in range(0, HALF, 96):
                rows = pl.ds(at + k, 96)
                p0[color, rows, :] = (
                    f32(p0[color, rows, :]) + f32(relay[color, way, k : k + 96, :])
                ).astype(jnp.bfloat16)
            nears[color, way, way] = send(
                p0.at[color, pl.ds(at, HALF)],
                near.at[color, way, pl.ds(HALF * way, HALF)],
                send1.at[color, 4 + way],
                recv1.at[color, 4 + way],
                along(ORDERS[color][0], step),
            )
    for color in range(3):
        first[color, 0].wait_recv()

    second = {}
    for color in range(3):
        for way in range(2):
            for half in range(2):
                nears[color, way, half].wait_recv()
        at = chunk_at(color, 0)
        for k in range(0, CHUNK, 96):
            rows = pl.ds(at + k, 96)
            value = part[color, rows, :] + f32(rx0[color, rows, :])
            value += f32(near[color, 0, k : k + 96, :]) + f32(near[color, 1, k : k + 96, :])
            p1[color, k : k + 96, :] = value.astype(jnp.bfloat16)
        dim = ORDERS[color][1]
        for step in (2, 1, 3):
            at = pl.multiple_of(((here[dim] + step) % 4) * 96, 96)
            second[color, step] = send(
                p1.at[color, pl.ds(at, 96)],
                rx2.at[color, step - 1],
                send2.at[color, step - 1],
                recv2.at[color, step - 1],
                along(dim, step),
            )
    third = {}
    for color in range(3):
        dim = ORDERS[color][1]
        value = f32(p1[color, pl.ds(pl.multiple_of(here[dim] * 96, 96), 96), :])
        for step in (1, 2, 3):
            second[color, step].wait_recv()
            value += f32(rx2[color, step - 1])
        for t in range(4):
            p2[color, t] = value[24 * t : 24 * t + 24].astype(jnp.bfloat16)
        dim = ORDERS[color][2]
        for step in (2, 1, 3):
            third[color, step] = send(
                p2.at[color, (here[dim] + step) % 4],
                rx3.at[color, step - 1],
                send3.at[color, step - 1],
                recv3.at[color, step - 1],
                along(dim, step),
            )
    for copy in columns:
        copy.wait()
    parts = []
    for color in range(3):
        value = f32(p2[color, here[ORDERS[color][2]]])
        for step in (1, 2, 3):
            third[color, step].wait_recv()
            value += f32(rx3[color, step - 1])
        parts.append(value)
    s_all[grp] = jnp.concatenate(parts, axis=0).astype(jnp.bfloat16)
    fourth = {}
    for r in (3, 2, 1):
        fourth[r] = send(
            s_all.at[grp], s_all.at[grp], send4.at[r - 1], recv4.at[r - 1], grp_peer(r)
        )

    def dot(a, b, dims=(((1,), (0,)), ((), ()))):
        return lax.dot_general(a, b, dims, preferred_element_type=jnp.float32)

    def matches(shape, row_of, lane_of):
        return jnp.where(row_of(iota(shape, 0)) == lane_of(iota(shape, 1)), 1.0, 0.0)

    def cos_at(k):
        size = jnp.abs(k - 32)
        return jnp.where(size == 32, 63, size)

    def sin_at(k):
        size = jnp.abs(k - 32)
        return jnp.where(size == 0, -1, jnp.where(size == 32, 64, size + 31))

    row = iota((128, 128), 0)
    lane = iota((128, 128), 1)
    ky = 2 * (row & 31) + ((row >> 5) & 1)
    ysel = jnp.where(
        row < 64,
        jnp.where(cos_at(ky) == lane, 1.0, 0.0),
        jnp.where(sin_at(ky) == lane, jnp.where(ky < 32, -1.0, 1.0), 0.0),
    ).astype(jnp.bfloat16)
    kx = lane & 63
    same = (row >> 6) == (lane >> 6)
    xc = jnp.where(same & (cos_at(kx) == (row & 63)), 1.0, 0.0)
    xs = jnp.where(same & (sin_at(kx) == (row & 63)), jnp.where(kx < 32, -1.0, 1.0), 0.0)
    xsel = jnp.concatenate([xc, xs], axis=1).astype(jnp.bfloat16)
    srow, slane = iota((32, 512), 0), iota((32, 512), 1)
    at = (srow & 7) - 1
    spot = jnp.where(
        ((srow >> 3) == (slane >> 7)) & (at >= 0) & (at < 2) & ((slane & 127) == at * 64), 1.0, 0.0
    ).astype(jnp.bfloat16)
    frow, flane = iota((32, 128), 0), iota((32, 128), 1)
    fy = f32(2 * frow + (flane >> 6) - 32)
    fx = f32((flane & 63) - 32)
    filt = jnp.exp(-(fy * fy + fx * fx) / (BAND * BAND / 2.0))
    bits = iota((8, 128), 1) - 65
    weight = jnp.where((bits >= 0) & (bits < 12), f32(1 << jnp.clip(bits, 0, 12)), 0.0)

    for r in (1, 2, 3):
        fourth[r].wait_recv()
    blocks = [s_all[g] for g in range(4)]
    y = dot(ysel[:, :72], jnp.concatenate(blocks, axis=1)).astype(jnp.bfloat16)
    y = jnp.concatenate([y[:, 128 * g : 128 * g + 128] for g in range(4)], axis=0)
    z = dot(y, xsel)
    extra = jnp.concatenate([b[64:72] for b in blocks], axis=0)
    side = dot(ysel, extra, (((1,), (1,)), ((), ()))).astype(jnp.bfloat16)
    side = dot(side, spot)
    half = iota((32, 128), 1) < 64
    for g in range(4):
        rc = z[128 * g : 128 * g + 128, :128]
        rs = z[128 * g : 128 * g + 128, 128:]
        sg = side[:, 128 * g : 128 * g + 128]
        members = jnp.sum(f32(blocks[g][64:72]) * weight, axis=1, keepdims=True)
        planes = (rc[:64] - rs[64:] + sg[64:], sg[:64] - rc[64:] - rs[:64])
        for j in range(2):
            scale = filt / (members[1 + j : 2 + j] + ridge)
            for p in range(2):
                even, odd = planes[p][:32], planes[p][32:]
                if j == 0:
                    odd = pltpu.roll(odd, 64, 1)
                else:
                    even = pltpu.roll(even, 64, 1)
                value = jnp.where(half, even, odd) * scale
                final[g, j, p] = value
                gathered[pl.ds(256 * p + 2 * g + j, 32, stride=8), :] = f32(
                    value.astype(jnp.bfloat16)
                )
    avg_ref[...] = final[grp]

    blocks_of = nexts.reshape(32, 512, 128)
    energy = jnp.zeros((8, 128), jnp.float32)
    inner = jnp.zeros((512, 16), jnp.float32)
    for t in range(0, 32, 2):
        sides = []
        for u in (t, t + 1):
            re = gathered[8 * u : 8 * u + 8, :]
            im = gathered[256 + 8 * u : 264 + 8 * u, :]
            energy += re * re + im * im
            sides.append(jnp.concatenate([re, im], axis=0).astype(jnp.bfloat16))
        inner += dot(
            jnp.concatenate([blocks_of[t], blocks_of[t + 1]], axis=1),
            jnp.concatenate(sides, axis=1),
            (((1,), (1,)), ((), ())),
        )
    products[:, 0:16] = inner
    both = products[pl.ds(0, 256, stride=2), :] + pltpu.roll(
        products[pl.ds(1, 256, stride=2), :], 120, 1
    )
    energy = jnp.sum(energy, axis=1, keepdims=True)
    score_ref[...] = (both.T[:8] - 0.5 * energy) / BAND
    for copy in started:
        copy.wait_send()


def reduce_classes(acc, meta, next_block):
    vmem = pl.BlockSpec(memory_space=pltpu.VMEM)
    bf16 = jnp.bfloat16
    return pl.pallas_call(
        reduce_kernel,
        out_shape=(
            jax.ShapeDtypeStruct((2, 2, 32, 128), jnp.float32),
            jax.ShapeDtypeStruct((8, 256), jnp.float32),
        ),
        in_specs=[vmem, vmem, pl.BlockSpec(memory_space=pl.ANY)],
        out_specs=(vmem, vmem),
        scratch_shapes=[
            pltpu.VMEM((32, 256, 2, 128), bf16),
            pltpu.VMEM((64, PIX, 128), bf16),
            pltpu.VMEM((PIX, 128), jnp.float32),
            pltpu.VMEM((PIX, 128), jnp.float32),
            pltpu.VMEM((3, 1536, 128), jnp.float32),
            pltpu.VMEM((3, 1536, 128), bf16),
            pltpu.VMEM((3, 1536, 128), bf16),
            pltpu.VMEM((3, 1536, 128), bf16),
            pltpu.VMEM((3, 2, HALF, 128), bf16),
            pltpu.VMEM((3, 2, CHUNK, 128), bf16),
            pltpu.VMEM((3, CHUNK, 128), bf16),
            pltpu.VMEM((3, 3, 96, 128), bf16),
            pltpu.VMEM((3, 4, 24, 128), bf16),
            pltpu.VMEM((3, 3, 24, 128), bf16),
            pltpu.VMEM((4, 72, 128), bf16),
            pltpu.VMEM((2 * PIX, 256), bf16),
            pltpu.VMEM((4, 2, 2, 32, 128), jnp.float32),
            pltpu.VMEM((512, 128), jnp.float32),
            pltpu.VMEM((512, 128), jnp.float32),
            pltpu.SemaphoreType.DMA((32,)),
            pltpu.SemaphoreType.DMA((3, 4)),
            pltpu.SemaphoreType.DMA((3, 4)),
            pltpu.SemaphoreType.DMA((3, 6)),
            pltpu.SemaphoreType.DMA((3, 6)),
            pltpu.SemaphoreType.DMA((3, 3)),
            pltpu.SemaphoreType.DMA((3, 3)),
            pltpu.SemaphoreType.DMA((3, 3)),
            pltpu.SemaphoreType.DMA((3, 3)),
            pltpu.SemaphoreType.DMA((3,)),
            pltpu.SemaphoreType.DMA((3,)),
        ],
        compiler_params=pltpu.CompilerParams(
            collective_id=0, has_side_effects=True, vmem_limit_bytes=24 << 20
        ),
        name="reduce_classes",
    )(acc, meta, next_block)


def body(images, shifts, class_ids, next_block):
    meta = jnp.concatenate([shifts.T, class_ids[None, :]], axis=0)
    averages, scores = reduce_classes(class_images(images, meta), meta, next_block)
    return (averages.reshape(2, 2, BAND * BAND), scores)


def solution(mesh):
    placed = (
        P(("dp", "grp"), None, None),
        P(("dp", "grp"), None),
        P(("dp", "grp")),
        P("grp", None, None),
    )
    return jax.shard_map(
        body,
        mesh=mesh,
        in_specs=placed,
        out_specs=(P(("dp", "grp"), None, None), P("dp", "grp")),
        check_vma=False,
    )
```

```python
import math

import jax
import jax.numpy as jnp
from jax import lax
from jax.experimental import pallas as pl
from jax.experimental.pallas import tpu as pltpu
from jax.sharding import PartitionSpec as P

PIX = 128
BAND = 64
CLASSES = 256
REACH = 16
ROWS = PIX + 2 * REACH
OUT_ROWS = 72
STEP = 32
BATCH = 32
ridge = 4.0


def iota(shape, axis):
    return lax.broadcasted_iota(jnp.int32, shape, axis)


def wave(position, b):
    is_sin = ((b >= 32) & (b < 63)) | (b == 64)
    freq = jnp.where(b < 32, b, jnp.where(b < 63, b - 31, 32))
    residue = (position * freq - jnp.where(is_sin, 32, 0)) & (PIX - 1)
    value = jnp.cos(residue.astype(jnp.float32) * (2.0 * math.pi / PIX))
    return jnp.where(b <= 64, value * (1.0 / math.sqrt(PIX)), 0.0)


def class_kernel(meta_ref, img_hbm, acc, imgs, img_sem):
    count = imgs.shape[0]

    def chunk(k):
        at = pl.ds(k * STEP, STEP)
        return pltpu.make_async_copy(img_hbm.at[at], imgs.at[at], img_sem.at[k])

    for k in range(count // STEP):
        chunk(k).start()

    flat = wave(iota((PIX, 128), 0), iota((PIX, 128), 1))
    acc[CLASSES, 0:PIX, :] = flat
    acc[CLASSES + 1, 0:OUT_ROWS, :] = wave(iota((OUT_ROWS, PIX), 1), iota((OUT_ROWS, PIX), 0))
    lane = iota((PIX, 128), 1)
    low = jnp.where(lane < 64, flat, 0.0)
    last = wave(iota((PIX, 128), 0), jnp.full((PIX, 128), 64, jnp.int32))
    for j in range(2):
        acc[CLASSES + 2 + j, 0:PIX, :] = pltpu.roll(low, 64 * j, 1)
        acc[CLASSES + 4 + j, 0:PIX, :] = jnp.where(lane % 2 == j, last, 0.0)

    def clear(c, carry):
        acc[c] = jnp.zeros((ROWS, PIX), jnp.float32)
        return carry

    lax.fori_loop(0, CLASSES, clear, 0, unroll=4)

    def add_chunk(k, carry):
        chunk(k).wait()

        def add_image(n, inner):
            i = k * STEP + n
            row = meta_ref[1, i] + REACH
            moved = pltpu.roll(imgs[i].astype(jnp.float32), meta_ref[0, i] & (PIX - 1), 1)
            acc[meta_ref[2, i], pl.ds(row, PIX), :] += moved
            return inner

        return lax.fori_loop(0, STEP, add_image, carry, unroll=32)

    lax.fori_loop(0, count // STEP, add_chunk, 0)


def class_images(images, meta):
    return pl.pallas_call(
        class_kernel,
        out_shape=pltpu.VMEM((CLASSES + 6, ROWS, PIX), jnp.float32),
        in_specs=[
            pl.BlockSpec(memory_space=pltpu.SMEM),
            pl.BlockSpec(memory_space=pl.ANY),
        ],
        out_specs=pl.BlockSpec(memory_space=pltpu.VMEM),
        scratch_shapes=[
            pltpu.VMEM(images.shape, jnp.bfloat16),
            pltpu.SemaphoreType.DMA((images.shape[0] // STEP,)),
        ],
        compiler_params=pltpu.CompilerParams(vmem_limit_bytes=20 << 20),
        name="class_images",
    )(meta, images)


ORDERS = ((0, 1, 2), (1, 2, 0), (2, 0, 1))
CHUNK = 384
HALF = 192
MESH_ID = pl.DeviceIdType.MESH


def reduce_kernel(
    acc,
    meta_ref,
    next_ref,
    avg_ref,
    score_ref,
    nexts,
    x2,
    edge,
    side_rows,
    part,
    outgoing,
    rx0,
    p0,
    relay,
    near,
    p1,
    rx2,
    p2,
    rx3,
    s_all,
    w1_ref,
    final,
    gathered,
    products,
    send0,
    recv0,
    send1,
    recv1,
    send2,
    recv2,
    send3,
    recv3,
    send4,
    recv4,
):
    dp = lax.axis_index("dp")
    grp = lax.axis_index("grp")
    core = grp % 2
    here = (dp // 8, (grp // 2) * 2 + (dp // 4) % 2, dp % 4)

    def device(spot, on_core):
        x, y, z = spot
        return {"dp": (x * 2 + y % 2) * 4 + z, "grp": (y // 2) * 2 + on_core}

    def along(dim, step):
        spot = list(here)
        spot[dim] = (spot[dim] + step) % 4
        return device(spot, core)

    partner = {"dp": dp, "grp": grp + 1 - 2 * core}

    def grp_peer(r):
        low = (grp % 2 + r % 2) % 2
        high = (grp // 2 + r // 2) % 2
        return {"dp": dp, "grp": high * 2 + low}

    def flatten(lo, hi):
        def one(g, carry):
            block = next_ref[pl.ds(g * 8, 8)]
            nexts[pl.ds(pl.multiple_of(g * 16, 16), 16), :] = block.reshape(16, block.shape[2])
            return carry

        lax.fori_loop(lo, hi, one, 0)

    barrier = pltpu.get_barrier_semaphore()
    peers = [partner, grp_peer(3)] + [along(d, s) for d in range(3) for s in (1, 2, 3)]
    for peer in peers:
        pl.semaphore_signal(barrier, inc=1, device_id=peer, device_id_type=MESH_ID)
    started = []

    def send(src, dst, ssem, rsem, where):
        copy = pltpu.make_async_remote_copy(
            src_ref=src,
            dst_ref=dst,
            send_sem=ssem,
            recv_sem=rsem,
            device_id=where,
            device_id_type=MESH_ID,
        )
        copy.start()
        started.append(copy)
        return copy

    def chunk_at(color, step):
        return pl.multiple_of(((here[ORDERS[color][0]] + step) % 4) * CHUNK, CHUNK)

    lane128 = iota((PIX, 128), 1)
    byc = acc[CLASSES, 0:PIX, :].astype(jnp.bfloat16)
    byr = acc[CLASSES + 1, 0:OUT_ROWS, :].astype(jnp.bfloat16)
    for j in range(2):
        for h in range(2):
            w1_ref[PIX * j : PIX * j + PIX, 128 * h : 128 * h + 128] = acc[
                CLASSES + 2 + 2 * h + j, 0:PIX, :
            ].astype(jnp.bfloat16)
    lane_pair = lane128 // 2

    def folded(c):
        return jnp.concatenate(
            [
                acc[c, 16:32, :] + acc[c, 144:160, :],
                acc[c, 32:128, :],
                acc[c, 128:144, :] + acc[c, 0:16, :],
            ],
            axis=0,
        ).astype(jnp.bfloat16)

    def transform(on_core):
        def columns_of(p, carry):
            chip = p * BATCH
            lhs = []
            for k in range(BATCH):
                c = (chip + k) * 4 + 2 * on_core
                lhs.append(jnp.concatenate([folded(c), folded(c + 1)], axis=1))
            got = jnp.dot(
                jnp.concatenate(lhs, axis=0), w1_ref[...], preferred_element_type=jnp.float32
            )
            for k in range(BATCH):
                mine = got[PIX * k : PIX * k + PIX]
                x2[chip + k] = mine[:, :128].astype(jnp.bfloat16)
                pltpu.store(edge, mine[:, 128:], mask=lane_pair == chip + k)
            return carry

        lax.fori_loop(0, 64 // BATCH, columns_of, 0)
        side = lax.dot_general(
            edge[...].astype(jnp.bfloat16),
            byc,
            (((0,), (0,)), ((), ())),
            preferred_element_type=jnp.float32,
        )
        row = iota((128, meta_ref.shape[1]), 0)
        cls = (row // 2) * 4 + 2 * on_core + row % 2
        tally = jnp.sum(
            jnp.where(cls == meta_ref[2:3, :], 1.0, 0.0), axis=1, keepdims=True
        ).astype(jnp.int32)
        bit = lane128 - 65
        tally = jnp.where((bit >= 0) & (bit < 12), (tally >> jnp.clip(bit, 0, 12)) & 1, 0)
        side_rows[...] = side + tally.astype(jnp.float32)

        def rows_of(m, carry):
            eight = side_rows[pl.ds(pl.multiple_of(m * 8, 8), 8), :]
            sub = iota((8, 128), 0)
            place = (sub == 1) | (sub == 2)
            for k in range(0, 4, 2):
                q = m * 4 + k
                got = jnp.dot(
                    byr,
                    jnp.concatenate([x2[q], x2[q + 1]], axis=1),
                    preferred_element_type=jnp.float32,
                )
                for n in range(2):
                    q = m * 4 + k + n
                    block = got[:, 128 * n : 128 * n + 128]
                    extra = jnp.where(place, pltpu.roll(eight, (1 - 2 * (k + n)) % 8, 0), 0.0)
                    block = jnp.concatenate([block[:64], block[64:] + extra], axis=0)
                    x, y, z = q // 16, (q % 2) * 2 + (q // 8) % 2, (q // 2) % 4
                    spots = (x * 16 + y * 4 + z, y * 16 + z * 4 + x, z * 16 + x * 4 + y)
                    for color in range(3):
                        at = pl.multiple_of(spots[color] * 24, 8)
                        part[color, pl.ds(at, 24), :] = block[24 * color : 24 * color + 24]
            return carry

        lax.fori_loop(0, 16, rows_of, 0, unroll=16)

    transform(1 - core)
    first = {}
    for step in (2, 1, 3, 0):
        for color in range(3):
            at = chunk_at(color, step)
            for k in range(0, CHUNK, 128):
                rows = pl.ds(at + k, 128)
                outgoing[color, rows, :] = part[color, rows, :].astype(jnp.bfloat16)
    pl.semaphore_wait(barrier, len(peers))
    for step in (2, 1, 3, 0):
        for color in range(3):
            at = chunk_at(color, step)
            first[color, step] = send(
                outgoing.at[color, pl.ds(at, CHUNK)],
                rx0.at[color, pl.ds(at, CHUNK)],
                send0.at[color, step],
                recv0.at[color, step],
                partner,
            )
    transform(core)

    def f32(value):
        return value.astype(jnp.float32)

    def add_first(color, step):
        first[color, step].wait_recv()
        at = chunk_at(color, step)
        for k in range(0, CHUNK, 128):
            rows = pl.ds(at + k, 128)
            p0[color, rows, :] = (part[color, rows, :] + f32(rx0[color, rows, :])).astype(
                jnp.bfloat16
            )

    relays, nears = {}, {}
    for color in range(3):
        add_first(color, 2)
        at = chunk_at(color, 2)
        dim = ORDERS[color][0]
        for way, step in enumerate((1, 3)):
            relays[color, way] = send(
                p0.at[color, pl.ds(at + HALF * way, HALF)],
                relay.at[color, way],
                send1.at[color, way],
                recv1.at[color, way],
                along(dim, step),
            )
    for way, step in enumerate((1, 3)):
        for color in range(3):
            add_first(color, step)
            at = chunk_at(color, step)
            half = 1 - way
            nears[color, way, half] = send(
                p0.at[color, pl.ds(at + HALF * half, HALF)],
                near.at[color, way, pl.ds(HALF * half, HALF)],
                send1.at[color, 2 + way],
                recv1.at[color, 2 + way],
                along(ORDERS[color][0], step),
            )
    flatten(0, 8)
    for color in range(3):
        for way, step in enumerate((1, 3)):
            relays[color, way].wait_recv()
            at = chunk_at(color, step) + HALF * way
            for k in range(0, HALF, 96):
                rows = pl.ds(at + k, 96)
                p0[color, rows, :] = (
                    f32(p0[color, rows, :]) + f32(relay[color, way, k : k + 96, :])
                ).astype(jnp.bfloat16)
            nears[color, way, way] = send(
                p0.at[color, pl.ds(at, HALF)],
                near.at[color, way, pl.ds(HALF * way, HALF)],
                send1.at[color, 4 + way],
                recv1.at[color, 4 + way],
                along(ORDERS[color][0], step),
            )
    flatten(8, 17)
    for color in range(3):
        first[color, 0].wait_recv()

    second = {}
    for color in range(3):
        for way in range(2):
            for half in range(2):
                nears[color, way, half].wait_recv()
        at = chunk_at(color, 0)
        for k in range(0, CHUNK, 96):
            rows = pl.ds(at + k, 96)
            value = part[color, rows, :] + f32(rx0[color, rows, :])
            value += f32(near[color, 0, k : k + 96, :]) + f32(near[color, 1, k : k + 96, :])
            p1[color, k : k + 96, :] = value.astype(jnp.bfloat16)
        dim = ORDERS[color][1]
        for step in (2, 1, 3):
            at = pl.multiple_of(((here[dim] + step) % 4) * 96, 96)
            second[color, step] = send(
                p1.at[color, pl.ds(at, 96)],
                rx2.at[color, step - 1],
                send2.at[color, step - 1],
                recv2.at[color, step - 1],
                along(dim, step),
            )
    flatten(17, 25)
    third = {}
    for color in range(3):
        dim = ORDERS[color][1]
        value = f32(p1[color, pl.ds(pl.multiple_of(here[dim] * 96, 96), 96), :])
        for step in (1, 2, 3):
            second[color, step].wait_recv()
            value += f32(rx2[color, step - 1])
        for t in range(4):
            p2[color, t] = value[24 * t : 24 * t + 24].astype(jnp.bfloat16)
        dim = ORDERS[color][2]
        for step in (2, 1, 3):
            third[color, step] = send(
                p2.at[color, (here[dim] + step) % 4],
                rx3.at[color, step - 1],
                send3.at[color, step - 1],
                recv3.at[color, step - 1],
                along(dim, step),
            )
    flatten(25, 32)
    parts = []
    for color in range(3):
        value = f32(p2[color, here[ORDERS[color][2]]])
        for step in (1, 2, 3):
            third[color, step].wait_recv()
            value += f32(rx3[color, step - 1])
        parts.append(value)
    s_all[grp] = jnp.concatenate(parts, axis=0).astype(jnp.bfloat16)
    fourth = {}
    for r in (3, 2, 1):
        fourth[r] = send(
            s_all.at[grp], s_all.at[grp], send4.at[r - 1], recv4.at[r - 1], grp_peer(r)
        )

    def dot(a, b, dims=(((1,), (0,)), ((), ()))):
        return lax.dot_general(a, b, dims, preferred_element_type=jnp.float32)

    def matches(shape, row_of, lane_of):
        return jnp.where(row_of(iota(shape, 0)) == lane_of(iota(shape, 1)), 1.0, 0.0)

    def cos_at(k):
        size = jnp.abs(k - 32)
        return jnp.where(size == 32, 63, size)

    def sin_at(k):
        size = jnp.abs(k - 32)
        return jnp.where(size == 0, -1, jnp.where(size == 32, 64, size + 31))

    row = iota((128, 128), 0)
    lane = iota((128, 128), 1)
    ky = 2 * (row & 31) + ((row >> 5) & 1)
    ysel = jnp.where(
        row < 64,
        jnp.where(cos_at(ky) == lane, 1.0, 0.0),
        jnp.where(sin_at(ky) == lane, jnp.where(ky < 32, -1.0, 1.0), 0.0),
    ).astype(jnp.bfloat16)
    kx = lane & 63
    same = (row >> 6) == (lane >> 6)
    xc = jnp.where(same & (cos_at(kx) == (row & 63)), 1.0, 0.0)
    xs = jnp.where(same & (sin_at(kx) == (row & 63)), jnp.where(kx < 32, -1.0, 1.0), 0.0)
    xsel = jnp.concatenate([xc, xs], axis=1).astype(jnp.bfloat16)
    srow, slane = iota((32, 512), 0), iota((32, 512), 1)
    at = (srow & 7) - 1
    spot = jnp.where(
        ((srow >> 3) == (slane >> 7)) & (at >= 0) & (at < 2) & ((slane & 127) == at * 64), 1.0, 0.0
    ).astype(jnp.bfloat16)
    frow, flane = iota((32, 128), 0), iota((32, 128), 1)
    fy = f32(2 * frow + (flane >> 6) - 32)
    fx = f32((flane & 63) - 32)
    filt = jnp.exp(-(fy * fy + fx * fx) / (BAND * BAND / 2.0))
    bits = iota((8, 128), 1) - 65
    weight = jnp.where((bits >= 0) & (bits < 12), f32(1 << jnp.clip(bits, 0, 12)), 0.0)

    for r in (1, 2, 3):
        fourth[r].wait_recv()
    blocks = [s_all[g] for g in range(4)]
    y = dot(ysel[:, :72], jnp.concatenate(blocks, axis=1)).astype(jnp.bfloat16)
    y = jnp.concatenate([y[:, 128 * g : 128 * g + 128] for g in range(4)], axis=0)
    z = dot(y, xsel)
    extra = jnp.concatenate([b[64:72] for b in blocks], axis=0)
    side = dot(ysel, extra, (((1,), (1,)), ((), ()))).astype(jnp.bfloat16)
    side = dot(side, spot)
    half = iota((32, 128), 1) < 64
    for g in range(4):
        rc = z[128 * g : 128 * g + 128, :128]
        rs = z[128 * g : 128 * g + 128, 128:]
        sg = side[:, 128 * g : 128 * g + 128]
        members = jnp.sum(f32(blocks[g][64:72]) * weight, axis=1, keepdims=True)
        planes = (rc[:64] - rs[64:] + sg[64:], sg[:64] - rc[64:] - rs[:64])
        for j in range(2):
            scale = filt / (members[1 + j : 2 + j] + ridge)
            for p in range(2):
                even, odd = planes[p][:32], planes[p][32:]
                if j == 0:
                    odd = pltpu.roll(odd, 64, 1)
                else:
                    even = pltpu.roll(even, 64, 1)
                value = jnp.where(half, even, odd) * scale
                final[g, j, p] = value
                gathered[pl.ds(256 * p + 2 * g + j, 32, stride=8), :] = f32(
                    value.astype(jnp.bfloat16)
                )
    avg_ref[...] = final[grp]

    energy = jnp.zeros((8, 128), jnp.float32)
    inner = jnp.zeros((512, 16), jnp.float32)
    for t in range(0, 32, 2):
        sides = []
        for u in (t, t + 1):
            re = gathered[8 * u : 8 * u + 8, :]
            im = gathered[256 + 8 * u : 264 + 8 * u, :]
            energy += re * re + im * im
            sides.append(jnp.concatenate([re, im], axis=0).astype(jnp.bfloat16))
        inner += dot(
            nexts[:, 128 * t : 128 * t + 256],
            jnp.concatenate(sides, axis=1),
            (((1,), (1,)), ((), ())),
        )
    products[:, 0:16] = inner
    both = products[pl.ds(0, 256, stride=2), :] + pltpu.roll(
        products[pl.ds(1, 256, stride=2), :], 120, 1
    )
    energy = jnp.sum(energy, axis=1, keepdims=True)
    score_ref[...] = (both.T[:8] - 0.5 * energy) / BAND
    for copy in started:
        copy.wait_send()


def reduce_classes(acc, meta, next_block):
    vmem = pl.BlockSpec(memory_space=pltpu.VMEM)
    bf16 = jnp.bfloat16
    return pl.pallas_call(
        reduce_kernel,
        out_shape=(
            jax.ShapeDtypeStruct((2, 2, 32, 128), jnp.float32),
            jax.ShapeDtypeStruct((8, 256), jnp.float32),
        ),
        in_specs=[vmem] * 3,
        out_specs=(vmem, vmem),
        scratch_shapes=[
            pltpu.VMEM((512, 4096), bf16),
            pltpu.VMEM((64, PIX, 128), bf16),
            pltpu.VMEM((PIX, 128), jnp.float32),
            pltpu.VMEM((PIX, 128), jnp.float32),
            pltpu.VMEM((3, 1536, 128), jnp.float32),
            pltpu.VMEM((3, 1536, 128), bf16),
            pltpu.VMEM((3, 1536, 128), bf16),
            pltpu.VMEM((3, 1536, 128), bf16),
            pltpu.VMEM((3, 2, HALF, 128), bf16),
            pltpu.VMEM((3, 2, CHUNK, 128), bf16),
            pltpu.VMEM((3, CHUNK, 128), bf16),
            pltpu.VMEM((3, 3, 96, 128), bf16),
            pltpu.VMEM((3, 4, 24, 128), bf16),
            pltpu.VMEM((3, 3, 24, 128), bf16),
            pltpu.VMEM((4, 72, 128), bf16),
            pltpu.VMEM((2 * PIX, 256), bf16),
            pltpu.VMEM((4, 2, 2, 32, 128), jnp.float32),
            pltpu.VMEM((512, 128), jnp.float32),
            pltpu.VMEM((512, 128), jnp.float32),
            pltpu.SemaphoreType.DMA((3, 4)),
            pltpu.SemaphoreType.DMA((3, 4)),
            pltpu.SemaphoreType.DMA((3, 6)),
            pltpu.SemaphoreType.DMA((3, 6)),
            pltpu.SemaphoreType.DMA((3, 3)),
            pltpu.SemaphoreType.DMA((3, 3)),
            pltpu.SemaphoreType.DMA((3, 3)),
            pltpu.SemaphoreType.DMA((3, 3)),
            pltpu.SemaphoreType.DMA((3,)),
            pltpu.SemaphoreType.DMA((3,)),
        ],
        compiler_params=pltpu.CompilerParams(
            collective_id=0, has_side_effects=True, vmem_limit_bytes=24 << 20
        ),
        name="reduce_classes",
    )(acc, meta, next_block)


def body(images, shifts, class_ids, next_block):
    meta = jnp.concatenate([shifts.T, class_ids[None, :]], axis=0)
    averages, scores = reduce_classes(class_images(images, meta), meta, next_block)
    return (averages.reshape(2, 2, BAND * BAND), scores)


def solution(mesh):
    placed = (
        P(("dp", "grp"), None, None),
        P(("dp", "grp"), None),
        P(("dp", "grp")),
        P("grp", None, None),
    )
    return jax.shard_map(
        body,
        mesh=mesh,
        in_specs=placed,
        out_specs=(P(("dp", "grp"), None, None), P("dp", "grp")),
        check_vma=False,
    )
```

```python
import math

import jax
import jax.numpy as jnp
from jax import lax
from jax.experimental import pallas as pl
from jax.experimental.pallas import tpu as pltpu
from jax.sharding import PartitionSpec as P

PIX = 128
BAND = 64
CLASSES = 256
REACH = 16
ROWS = PIX + 2 * REACH
OUT_ROWS = 72
STEP = 64
BATCH = 32
ridge = 4.0


def iota(shape, axis):
    return lax.broadcasted_iota(jnp.int32, shape, axis)


def wave(position, b):
    is_sin = ((b >= 32) & (b < 63)) | (b == 64)
    freq = jnp.where(b < 32, b, jnp.where(b < 63, b - 31, 32))
    residue = (position * freq - jnp.where(is_sin, 32, 0)) & (PIX - 1)
    value = jnp.cos(residue.astype(jnp.float32) * (2.0 * math.pi / PIX))
    return jnp.where(b <= 64, value * (1.0 / math.sqrt(PIX)), 0.0)


def class_kernel(meta_ref, img_hbm, acc, imgs, img_sem):
    count = imgs.shape[0]

    def chunk(k):
        at = pl.ds(k * STEP, STEP)
        return pltpu.make_async_copy(img_hbm.at[at], imgs.at[at], img_sem.at[k])

    for k in range(count // STEP):
        chunk(k).start()

    flat = wave(iota((PIX, 128), 0), iota((PIX, 128), 1))
    acc[CLASSES, 0:PIX, :] = flat
    acc[CLASSES + 1, 0:OUT_ROWS, :] = wave(iota((OUT_ROWS, PIX), 1), iota((OUT_ROWS, PIX), 0))
    lane = iota((PIX, 128), 1)
    low = jnp.where(lane < 64, flat, 0.0)
    last = wave(iota((PIX, 128), 0), jnp.full((PIX, 128), 64, jnp.int32))
    for j in range(2):
        acc[CLASSES + 2 + j, 0:PIX, :] = pltpu.roll(low, 64 * j, 1)
        acc[CLASSES + 4 + j, 0:PIX, :] = jnp.where(lane % 2 == j, last, 0.0)

    def clear(c, carry):
        acc[c] = jnp.zeros((ROWS, PIX), jnp.float32)
        return carry

    lax.fori_loop(0, CLASSES, clear, 0, unroll=4)

    def add_chunk(k, carry):
        chunk(k).wait()

        def add_image(n, inner):
            i = k * STEP + n
            row = meta_ref[1, i] + REACH
            moved = pltpu.roll(imgs[i].astype(jnp.float32), meta_ref[0, i] & (PIX - 1), 1)
            acc[meta_ref[2, i], pl.ds(row, PIX), :] += moved
            return inner

        return lax.fori_loop(0, STEP, add_image, carry, unroll=64)

    lax.fori_loop(0, count // STEP, add_chunk, 0)


def class_images(images, meta):
    return pl.pallas_call(
        class_kernel,
        out_shape=pltpu.VMEM((CLASSES + 6, ROWS, PIX), jnp.float32),
        in_specs=[
            pl.BlockSpec(memory_space=pltpu.SMEM),
            pl.BlockSpec(memory_space=pl.ANY),
        ],
        out_specs=pl.BlockSpec(memory_space=pltpu.VMEM),
        scratch_shapes=[
            pltpu.VMEM(images.shape, jnp.bfloat16),
            pltpu.SemaphoreType.DMA((images.shape[0] // STEP,)),
        ],
        compiler_params=pltpu.CompilerParams(vmem_limit_bytes=20 << 20),
        name="class_images",
    )(meta, images)


PLANE = (10, 9, 11, 6, 14, 8, 2, 5, 7, 13, 15, 4, 12, 1, 3)
ORDERS = ((0, 1, 2), (1, 2, 0), (2, 0, 1))
CHUNK = 384
HALF = 192
MESH_ID = pl.DeviceIdType.MESH


def reduce_kernel(
    acc,
    meta_ref,
    next_ref,
    avg_ref,
    score_ref,
    nexts,
    x2,
    edge,
    side_rows,
    part,
    outgoing,
    rx0,
    p0,
    near,
    p1,
    rx2,
    s_all,
    w1_ref,
    final,
    gathered,
    products,
    send0,
    recv0,
    send1,
    recv1,
    send2,
    recv2,
    send4,
    recv4,
):
    dp = lax.axis_index("dp")
    grp = lax.axis_index("grp")
    core = grp % 2
    here = (dp // 8, (grp // 2) * 2 + (dp // 4) % 2, dp % 4)

    def device(spot, on_core):
        x, y, z = spot
        return {"dp": (x * 2 + y % 2) * 4 + z, "grp": (y // 2) * 2 + on_core}

    def along(dim, step):
        spot = list(here)
        spot[dim] = (spot[dim] + step) % 4
        return device(spot, core)

    def in_plane(color, hop):
        _, one, two = ORDERS[color]
        spot = list(here)
        spot[one] = (spot[one] + hop // 4) % 4
        spot[two] = (spot[two] + hop % 4) % 4
        return device(spot, core)

    def plane_at(color, hop):
        _, one, two = ORDERS[color]
        return (here[one] + hop // 4) % 4 * 4 + (here[two] + hop % 4) % 4

    partner = {"dp": dp, "grp": grp + 1 - 2 * core}

    def grp_peer(r):
        low = (grp % 2 + r % 2) % 2
        high = (grp // 2 + r // 2) % 2
        return {"dp": dp, "grp": high * 2 + low}

    def flatten(lo, hi):
        def one(g, carry):
            block = next_ref[pl.ds(g * 8, 8)]
            nexts[pl.ds(pl.multiple_of(g * 16, 16), 16), :] = block.reshape(16, block.shape[2])
            return carry

        lax.fori_loop(lo, hi, one, 0)

    barrier = pltpu.get_barrier_semaphore()
    peers = [partner, grp_peer(3)] + [along(d, s) for d in range(3) for s in (1, 2, 3)]
    peers += [in_plane(c, h) for c in range(3) for h in range(1, 16) if h // 4 and h % 4]
    for peer in peers:
        pl.semaphore_signal(barrier, inc=1, device_id=peer, device_id_type=MESH_ID)
    started = []

    def send(src, dst, ssem, rsem, where):
        copy = pltpu.make_async_remote_copy(
            src_ref=src,
            dst_ref=dst,
            send_sem=ssem,
            recv_sem=rsem,
            device_id=where,
            device_id_type=MESH_ID,
        )
        copy.start()
        started.append(copy)
        return copy

    def chunk_at(color, step):
        return pl.multiple_of(((here[ORDERS[color][0]] + step) % 4) * CHUNK, CHUNK)

    lane128 = iota((PIX, 128), 1)
    byc = acc[CLASSES, 0:PIX, :].astype(jnp.bfloat16)
    byr = acc[CLASSES + 1, 0:OUT_ROWS, :].astype(jnp.bfloat16)
    for j in range(2):
        for h in range(2):
            w1_ref[PIX * j : PIX * j + PIX, 128 * h : 128 * h + 128] = acc[
                CLASSES + 2 + 2 * h + j, 0:PIX, :
            ].astype(jnp.bfloat16)
    lane_pair = lane128 // 2

    def folded(c):
        return jnp.concatenate(
            [
                acc[c, 16:32, :] + acc[c, 144:160, :],
                acc[c, 32:128, :],
                acc[c, 128:144, :] + acc[c, 0:16, :],
            ],
            axis=0,
        ).astype(jnp.bfloat16)

    def transform(on_core):
        def columns_of(p, carry):
            chip = p * BATCH
            lhs = []
            for k in range(BATCH):
                c = (chip + k) * 4 + 2 * on_core
                lhs.append(jnp.concatenate([folded(c), folded(c + 1)], axis=1))
            got = jnp.dot(
                jnp.concatenate(lhs, axis=0), w1_ref[...], preferred_element_type=jnp.float32
            )
            for k in range(BATCH):
                mine = got[PIX * k : PIX * k + PIX]
                x2[chip + k] = mine[:, :128].astype(jnp.bfloat16)
                pltpu.store(edge, mine[:, 128:], mask=lane_pair == chip + k)
            return carry

        lax.fori_loop(0, 64 // BATCH, columns_of, 0)
        side = lax.dot_general(
            edge[...].astype(jnp.bfloat16),
            byc,
            (((0,), (0,)), ((), ())),
            preferred_element_type=jnp.float32,
        )
        row = iota((128, meta_ref.shape[1]), 0)
        cls = (row // 2) * 4 + 2 * on_core + row % 2
        tally = jnp.sum(
            jnp.where(cls == meta_ref[2:3, :], 1.0, 0.0), axis=1, keepdims=True
        ).astype(jnp.int32)
        bit = lane128 - 65
        tally = jnp.where((bit >= 0) & (bit < 12), (tally >> jnp.clip(bit, 0, 12)) & 1, 0)
        side_rows[...] = side + tally.astype(jnp.float32)

        def rows_of(m, carry):
            eight = side_rows[pl.ds(pl.multiple_of(m * 8, 8), 8), :]
            sub = iota((8, 128), 0)
            place = (sub == 1) | (sub == 2)
            for k in range(0, 4, 2):
                q = m * 4 + k
                got = jnp.dot(
                    byr,
                    jnp.concatenate([x2[q], x2[q + 1]], axis=1),
                    preferred_element_type=jnp.float32,
                )
                for n in range(2):
                    q = m * 4 + k + n
                    block = got[:, 128 * n : 128 * n + 128]
                    extra = jnp.where(place, pltpu.roll(eight, (1 - 2 * (k + n)) % 8, 0), 0.0)
                    block = jnp.concatenate([block[:64], block[64:] + extra], axis=0)
                    x, y, z = q // 16, (q % 2) * 2 + (q // 8) % 2, (q // 2) % 4
                    spots = (x * 16 + y * 4 + z, y * 16 + z * 4 + x, z * 16 + x * 4 + y)
                    for color in range(3):
                        at = pl.multiple_of(spots[color] * 24, 8)
                        part[color, pl.ds(at, 24), :] = block[24 * color : 24 * color + 24]
            return carry

        lax.fori_loop(0, 16, rows_of, 0, unroll=16)

    transform(1 - core)
    first = {}
    for step in (2, 1, 3, 0):
        for color in range(3):
            at = chunk_at(color, step)
            for k in range(0, CHUNK, 128):
                rows = pl.ds(at + k, 128)
                outgoing[color, rows, :] = part[color, rows, :].astype(jnp.bfloat16)
    pl.semaphore_wait(barrier, len(peers))
    for step in (2, 1, 3, 0):
        for color in range(3):
            at = chunk_at(color, step)
            first[color, step] = send(
                outgoing.at[color, pl.ds(at, CHUNK)],
                rx0.at[color, pl.ds(at, CHUNK)],
                send0.at[color, step],
                recv0.at[color, step],
                partner,
            )
    transform(core)

    def f32(value):
        return value.astype(jnp.float32)

    def add_first(color, step):
        first[color, step].wait_recv()
        at = chunk_at(color, step)
        for k in range(0, CHUNK, 128):
            rows = pl.ds(at + k, 128)
            p0[color, rows, :] = (part[color, rows, :] + f32(rx0[color, rows, :])).astype(
                jnp.bfloat16
            )

    nears = {}
    for step in (2, 1, 3):
        for color in range(3):
            add_first(color, step)
            nears[color, step] = send(
                p0.at[color, pl.ds(chunk_at(color, step), CHUNK)],
                near.at[color, step - 1],
                send1.at[color, step - 1],
                recv1.at[color, step - 1],
                along(ORDERS[color][0], step),
            )
    flatten(0, 17)
    for color in range(3):
        first[color, 0].wait_recv()

    second = {}
    for color in range(3):
        for step in (1, 2, 3):
            nears[color, step].wait_recv()
        at = chunk_at(color, 0)
        for k in range(0, CHUNK, 96):
            rows = pl.ds(at + k, 96)
            value = part[color, rows, :] + f32(rx0[color, rows, :])
            for step in range(3):
                value += f32(near[color, step, k : k + 96, :])
            for t in range(4):
                p1[color, k // 24 + t] = value[24 * t : 24 * t + 24].astype(jnp.bfloat16)
        for hop in PLANE:
            second[color, hop] = send(
                p1.at[color, plane_at(color, hop)],
                rx2.at[color, hop - 1],
                send2.at[color, hop - 1],
                recv2.at[color, hop - 1],
                in_plane(color, hop),
            )
    flatten(17, 32)
    fourth = {}
    for color in range(3):
        value = f32(p1[color, plane_at(color, 0)])
        for hop in PLANE:
            second[color, hop].wait_recv()
        for hop in range(1, 16):
            value += f32(rx2[color, hop - 1])
        s_all[grp, color] = value.astype(jnp.bfloat16)
        for r in (3, 2, 1):
            fourth[color, r] = send(
                s_all.at[grp, color],
                s_all.at[grp, color],
                send4.at[color, r - 1],
                recv4.at[color, r - 1],
                grp_peer(r),
            )

    def dot(a, b, dims=(((1,), (0,)), ((), ()))):
        return lax.dot_general(a, b, dims, preferred_element_type=jnp.float32)

    def matches(shape, row_of, lane_of):
        return jnp.where(row_of(iota(shape, 0)) == lane_of(iota(shape, 1)), 1.0, 0.0)

    def cos_at(k):
        size = jnp.abs(k - 32)
        return jnp.where(size == 32, 63, size)

    def sin_at(k):
        size = jnp.abs(k - 32)
        return jnp.where(size == 0, -1, jnp.where(size == 32, 64, size + 31))

    row = iota((128, 128), 0)
    lane = iota((128, 128), 1)
    ky = 2 * (row & 31) + ((row >> 5) & 1)
    ysel = jnp.where(
        row < 64,
        jnp.where(cos_at(ky) == lane, 1.0, 0.0),
        jnp.where(sin_at(ky) == lane, jnp.where(ky < 32, -1.0, 1.0), 0.0),
    ).astype(jnp.bfloat16)
    kx = lane & 63
    same = (row >> 6) == (lane >> 6)
    xc = jnp.where(same & (cos_at(kx) == (row & 63)), 1.0, 0.0)
    xs = jnp.where(same & (sin_at(kx) == (row & 63)), jnp.where(kx < 32, -1.0, 1.0), 0.0)
    xsel = jnp.concatenate([xc, xs], axis=1).astype(jnp.bfloat16)
    srow, slane = iota((32, 512), 0), iota((32, 512), 1)
    at = (srow & 7) - 1
    spot = jnp.where(
        ((srow >> 3) == (slane >> 7)) & (at >= 0) & (at < 2) & ((slane & 127) == at * 64), 1.0, 0.0
    ).astype(jnp.bfloat16)
    frow, flane = iota((32, 128), 0), iota((32, 128), 1)
    fy = f32(2 * frow + (flane >> 6) - 32)
    fx = f32((flane & 63) - 32)
    filt = jnp.exp(-(fy * fy + fx * fx) / (BAND * BAND / 2.0))
    bits = iota((8, 128), 1) - 65
    weight = jnp.where((bits >= 0) & (bits < 12), f32(1 << jnp.clip(bits, 0, 12)), 0.0)

    for color in range(3):
        for r in (1, 2, 3):
            fourth[color, r].wait_recv()
    blocks = [
        jnp.concatenate([f32(s_all[g, color]) for color in range(3)], axis=0).astype(jnp.bfloat16)
        for g in range(4)
    ]
    y = dot(ysel[:, :72], jnp.concatenate(blocks, axis=1)).astype(jnp.bfloat16)
    y = jnp.concatenate([y[:, 128 * g : 128 * g + 128] for g in range(4)], axis=0)
    z = dot(y, xsel)
    extra = jnp.concatenate([b[64:72] for b in blocks], axis=0)
    side = dot(ysel, extra, (((1,), (1,)), ((), ()))).astype(jnp.bfloat16)
    side = dot(side, spot)
    half = iota((32, 128), 1) < 64
    for g in range(4):
        rc = z[128 * g : 128 * g + 128, :128]
        rs = z[128 * g : 128 * g + 128, 128:]
        sg = side[:, 128 * g : 128 * g + 128]
        members = jnp.sum(f32(blocks[g][64:72]) * weight, axis=1, keepdims=True)
        planes = (rc[:64] - rs[64:] + sg[64:], sg[:64] - rc[64:] - rs[:64])
        for j in range(2):
            scale = filt / (members[1 + j : 2 + j] + ridge)
            for p in range(2):
                even, odd = planes[p][:32], planes[p][32:]
                if j == 0:
                    odd = pltpu.roll(odd, 64, 1)
                else:
                    even = pltpu.roll(even, 64, 1)
                value = jnp.where(half, even, odd) * scale
                final[g, j, p] = value
                gathered[pl.ds(256 * p + 2 * g + j, 32, stride=8), :] = f32(
                    value.astype(jnp.bfloat16)
                )
    avg_ref[...] = final[grp]

    energy = jnp.zeros((8, 128), jnp.float32)
    inner = jnp.zeros((512, 16), jnp.float32)
    for t in range(0, 32, 2):
        sides = []
        for u in (t, t + 1):
            re = gathered[8 * u : 8 * u + 8, :]
            im = gathered[256 + 8 * u : 264 + 8 * u, :]
            energy += re * re + im * im
            sides.append(jnp.concatenate([re, im], axis=0).astype(jnp.bfloat16))
        inner += dot(
            nexts[:, 128 * t : 128 * t + 256],
            jnp.concatenate(sides, axis=1),
            (((1,), (1,)), ((), ())),
        )
    products[:, 0:16] = inner
    both = products[pl.ds(0, 256, stride=2), :] + pltpu.roll(
        products[pl.ds(1, 256, stride=2), :], 120, 1
    )
    energy = jnp.sum(energy, axis=1, keepdims=True)
    score_ref[...] = (both.T[:8] - 0.5 * energy) / BAND
    for copy in started:
        copy.wait_send()


def reduce_classes(acc, meta, next_block):
    vmem = pl.BlockSpec(memory_space=pltpu.VMEM)
    bf16 = jnp.bfloat16
    return pl.pallas_call(
        reduce_kernel,
        out_shape=(
            jax.ShapeDtypeStruct((2, 2, 32, 128), jnp.float32),
            jax.ShapeDtypeStruct((8, 256), jnp.float32),
        ),
        in_specs=[vmem] * 3,
        out_specs=(vmem, vmem),
        scratch_shapes=[
            pltpu.VMEM((512, 4096), bf16),
            pltpu.VMEM((64, PIX, 128), bf16),
            pltpu.VMEM((PIX, 128), jnp.float32),
            pltpu.VMEM((PIX, 128), jnp.float32),
            pltpu.VMEM((3, 1536, 128), jnp.float32),
            pltpu.VMEM((3, 1536, 128), bf16),
            pltpu.VMEM((3, 1536, 128), bf16),
            pltpu.VMEM((3, 1536, 128), bf16),
            pltpu.VMEM((3, 3, CHUNK, 128), bf16),
            pltpu.VMEM((3, 16, 24, 128), bf16),
            pltpu.VMEM((3, 15, 24, 128), bf16),
            pltpu.VMEM((4, 3, 24, 128), bf16),
            pltpu.VMEM((2 * PIX, 256), bf16),
            pltpu.VMEM((4, 2, 2, 32, 128), jnp.float32),
            pltpu.VMEM((512, 128), jnp.float32),
            pltpu.VMEM((512, 128), jnp.float32),
            pltpu.SemaphoreType.DMA((3, 4)),
            pltpu.SemaphoreType.DMA((3, 4)),
            pltpu.SemaphoreType.DMA((3, 6)),
            pltpu.SemaphoreType.DMA((3, 6)),
            pltpu.SemaphoreType.DMA((3, 15)),
            pltpu.SemaphoreType.DMA((3, 15)),
            pltpu.SemaphoreType.DMA((3, 3)),
            pltpu.SemaphoreType.DMA((3, 3)),
        ],
        compiler_params=pltpu.CompilerParams(
            collective_id=0, has_side_effects=True, vmem_limit_bytes=24 << 20
        ),
        name="reduce_classes",
    )(acc, meta, next_block)


def body(images, shifts, class_ids, next_block):
    meta = jnp.concatenate([shifts.T, class_ids[None, :]], axis=0)
    averages, scores = reduce_classes(class_images(images, meta), meta, next_block)
    return (averages.reshape(2, 2, BAND * BAND), scores)


def solution(mesh):
    placed = (
        P(("dp", "grp"), None, None),
        P(("dp", "grp"), None),
        P(("dp", "grp")),
        P("grp", None, None),
    )
    return jax.shard_map(
        body,
        mesh=mesh,
        in_specs=placed,
        out_specs=(P(("dp", "grp"), None, None), P("dp", "grp")),
        check_vma=False,
    )
```

```python
import math

import jax
import jax.numpy as jnp
from jax import lax
from jax.experimental import pallas as pl
from jax.experimental.pallas import tpu as pltpu
from jax.sharding import PartitionSpec as P

PIX = 128
BAND = 64
CLASSES = 256
REACH = 16
ROWS = PIX + 2 * REACH
OUT_ROWS = 72
STEP = 128
BATCH = 32
ridge = 4.0


def iota(shape, axis):
    return lax.broadcasted_iota(jnp.int32, shape, axis)


def wave(position, b):
    is_sin = ((b >= 32) & (b < 63)) | (b == 64)
    freq = jnp.where(b < 32, b, jnp.where(b < 63, b - 31, 32))
    residue = (position * freq - jnp.where(is_sin, 32, 0)) & (PIX - 1)
    value = jnp.cos(residue.astype(jnp.float32) * (2.0 * math.pi / PIX))
    return jnp.where(b <= 64, value * (1.0 / math.sqrt(PIX)), 0.0)


def class_kernel(meta_ref, img_hbm, acc, imgs, img_sem):
    count = imgs.shape[0]

    def chunk(k):
        at = pl.ds(k * STEP, STEP)
        return pltpu.make_async_copy(img_hbm.at[at], imgs.at[at], img_sem.at[k])

    for k in range(count // STEP):
        chunk(k).start()

    flat = wave(iota((PIX, 128), 0), iota((PIX, 128), 1))
    acc[CLASSES, 0:PIX, :] = flat
    acc[CLASSES + 1, 0:OUT_ROWS, :] = wave(iota((OUT_ROWS, PIX), 1), iota((OUT_ROWS, PIX), 0))
    lane = iota((PIX, 128), 1)
    low = jnp.where(lane < 64, flat, 0.0)
    turn = iota((PIX, 128), 0) & 3
    last = jnp.where(turn == 1, 1.0, jnp.where(turn == 3, -1.0, 0.0)) * (1.0 / math.sqrt(PIX))
    for j in range(2):
        acc[CLASSES + 2 + j, 0:PIX, :] = pltpu.roll(low, 64 * j, 1)
        acc[CLASSES + 4 + j, 0:PIX, :] = jnp.where(lane % 2 == j, last, 0.0)

    def clear(c, carry):
        acc[c] = jnp.zeros((ROWS, PIX), jnp.float32)
        return carry

    lax.fori_loop(0, CLASSES, clear, 0, unroll=4)

    def add_chunk(k, carry):
        chunk(k).wait()

        def add_image(n, inner):
            i = k * STEP + n
            row = meta_ref[1, i] + REACH
            moved = pltpu.roll(imgs[i].astype(jnp.float32), meta_ref[0, i] & (PIX - 1), 1)
            acc[meta_ref[2, i], pl.ds(row, PIX), :] += moved
            return inner

        return lax.fori_loop(0, STEP, add_image, carry, unroll=128)

    lax.fori_loop(0, count // STEP, add_chunk, 0)


def class_images(images, meta):
    return pl.pallas_call(
        class_kernel,
        out_shape=pltpu.VMEM((CLASSES + 6, ROWS, PIX), jnp.float32),
        in_specs=[
            pl.BlockSpec(memory_space=pltpu.SMEM),
            pl.BlockSpec(memory_space=pl.ANY),
        ],
        out_specs=pl.BlockSpec(memory_space=pltpu.VMEM),
        scratch_shapes=[
            pltpu.VMEM(images.shape, jnp.bfloat16),
            pltpu.SemaphoreType.DMA((images.shape[0] // STEP,)),
        ],
        compiler_params=pltpu.CompilerParams(vmem_limit_bytes=20 << 20),
        name="class_images",
    )(meta, images)


PLANE = (10, 9, 11, 6, 14, 8, 2, 5, 7, 13, 15, 4, 12, 1, 3)
ORDERS = ((0, 1, 2), (1, 2, 0), (2, 0, 1))
CHUNK = 384
HALF = 192
MESH_ID = pl.DeviceIdType.MESH


def reduce_kernel(
    acc,
    meta_ref,
    next_ref,
    out_ref,
    x2,
    edge,
    side_rows,
    part,
    outgoing,
    rx0,
    p0,
    near,
    p1,
    rx2,
    s_all,
    w1_ref,
    send0,
    recv0,
    send1,
    recv1,
    send2,
    recv2,
    send4,
    recv4,
):
    dp = lax.axis_index("dp")
    grp = lax.axis_index("grp")
    core = grp % 2
    here = (dp // 8, (grp // 2) * 2 + (dp // 4) % 2, dp % 4)

    def device(spot, on_core):
        x, y, z = spot
        return {"dp": (x * 2 + y % 2) * 4 + z, "grp": (y // 2) * 2 + on_core}

    def along(dim, step):
        spot = list(here)
        spot[dim] = (spot[dim] + step) % 4
        return device(spot, core)

    def in_plane(color, hop):
        _, one, two = ORDERS[color]
        spot = list(here)
        spot[one] = (spot[one] + hop // 4) % 4
        spot[two] = (spot[two] + hop % 4) % 4
        return device(spot, core)

    def plane_at(color, hop):
        _, one, two = ORDERS[color]
        return (here[one] + hop // 4) % 4 * 4 + (here[two] + hop % 4) % 4

    partner = {"dp": dp, "grp": grp + 1 - 2 * core}

    def grp_peer(r):
        low = (grp % 2 + r % 2) % 2
        high = (grp // 2 + r // 2) % 2
        return {"dp": dp, "grp": high * 2 + low}

    def flatten(lo, hi):
        def one(g, carry):
            block = next_ref[pl.ds(g * 8, 8)]
            out_ref[pl.ds(pl.multiple_of(g * 16, 16), 16), :] = block.reshape(16, block.shape[2])
            return carry

        lax.fori_loop(lo, hi, one, 0)

    barrier = pltpu.get_barrier_semaphore()
    peers = [partner, grp_peer(3)] + [along(d, s) for d in range(3) for s in (1, 2, 3)]
    peers += [in_plane(c, h) for c in range(3) for h in range(1, 16) if h // 4 and h % 4]
    for peer in peers:
        pl.semaphore_signal(barrier, inc=1, device_id=peer, device_id_type=MESH_ID)
    started = []

    def send(src, dst, ssem, rsem, where):
        copy = pltpu.make_async_remote_copy(
            src_ref=src,
            dst_ref=dst,
            send_sem=ssem,
            recv_sem=rsem,
            device_id=where,
            device_id_type=MESH_ID,
        )
        copy.start()
        started.append(copy)
        return copy

    def chunk_at(color, step):
        return pl.multiple_of(((here[ORDERS[color][0]] + step) % 4) * CHUNK, CHUNK)

    lane128 = iota((PIX, 128), 1)
    byc = acc[CLASSES, 0:PIX, :].astype(jnp.bfloat16)
    byr = acc[CLASSES + 1, 0:OUT_ROWS, :].astype(jnp.bfloat16)
    for j in range(2):
        for h in range(2):
            w1_ref[PIX * j : PIX * j + PIX, 128 * h : 128 * h + 128] = acc[
                CLASSES + 2 + 2 * h + j, 0:PIX, :
            ].astype(jnp.bfloat16)
    lane_pair = lane128 // 2

    def folded(c):
        return jnp.concatenate(
            [
                acc[c, 16:32, :] + acc[c, 144:160, :],
                acc[c, 32:128, :],
                acc[c, 128:144, :] + acc[c, 0:16, :],
            ],
            axis=0,
        ).astype(jnp.bfloat16)

    def transform(on_core):
        def columns_of(p, carry):
            chip = p * BATCH
            lhs = []
            for k in range(BATCH):
                c = (chip + k) * 4 + 2 * on_core
                lhs.append(jnp.concatenate([folded(c), folded(c + 1)], axis=1))
            got = jnp.dot(
                jnp.concatenate(lhs, axis=0), w1_ref[...], preferred_element_type=jnp.float32
            )
            for k in range(BATCH):
                mine = got[PIX * k : PIX * k + PIX]
                x2[chip + k] = mine[:, :128].astype(jnp.bfloat16)
                pltpu.store(edge, mine[:, 128:], mask=lane_pair == chip + k)
            return carry

        lax.fori_loop(0, 64 // BATCH, columns_of, 0)
        side = lax.dot_general(
            edge[...].astype(jnp.bfloat16),
            byc,
            (((0,), (0,)), ((), ())),
            preferred_element_type=jnp.float32,
        )
        row = iota((128, meta_ref.shape[1]), 0)
        cls = (row // 2) * 4 + 2 * on_core + row % 2
        tally = jnp.sum(
            jnp.where(cls == meta_ref[2:3, :], 1.0, 0.0), axis=1, keepdims=True
        ).astype(jnp.int32)
        bit = lane128 - 65
        tally = jnp.where((bit >= 0) & (bit < 12), (tally >> jnp.clip(bit, 0, 12)) & 1, 0)
        side_rows[...] = side + tally.astype(jnp.float32)

        def rows_of(m, carry):
            eight = side_rows[pl.ds(pl.multiple_of(m * 8, 8), 8), :]
            sub = iota((8, 128), 0)
            place = (sub == 1) | (sub == 2)
            for k in range(0, 4, 2):
                q = m * 4 + k
                got = jnp.dot(
                    byr,
                    jnp.concatenate([x2[q], x2[q + 1]], axis=1),
                    preferred_element_type=jnp.float32,
                )
                for n in range(2):
                    q = m * 4 + k + n
                    block = got[:, 128 * n : 128 * n + 128]
                    extra = jnp.where(place, pltpu.roll(eight, (1 - 2 * (k + n)) % 8, 0), 0.0)
                    block = jnp.concatenate([block[:64], block[64:] + extra], axis=0)
                    x, y, z = q // 16, (q % 2) * 2 + (q // 8) % 2, (q // 2) % 4
                    spots = (x * 16 + y * 4 + z, y * 16 + z * 4 + x, z * 16 + x * 4 + y)
                    for color in range(3):
                        at = pl.multiple_of(spots[color] * 24, 8)
                        part[color, pl.ds(at, 24), :] = block[24 * color : 24 * color + 24]
            return carry

        lax.fori_loop(0, 16, rows_of, 0, unroll=16)

    transform(1 - core)
    first = {}
    for step in (2, 1, 3, 0):
        for color in range(3):
            at = chunk_at(color, step)
            for k in range(0, CHUNK, 128):
                rows = pl.ds(at + k, 128)
                outgoing[color, rows, :] = part[color, rows, :].astype(jnp.bfloat16)
    pl.semaphore_wait(barrier, len(peers))
    for step in (2, 1, 3, 0):
        for color in range(3):
            at = chunk_at(color, step)
            first[color, step] = send(
                outgoing.at[color, pl.ds(at, CHUNK)],
                rx0.at[color, pl.ds(at, CHUNK)],
                send0.at[color, step],
                recv0.at[color, step],
                partner,
            )
    transform(core)

    def f32(value):
        return value.astype(jnp.float32)

    def add_first(color, step):
        first[color, step].wait_recv()
        at = chunk_at(color, step)
        for k in range(0, CHUNK, 128):
            rows = pl.ds(at + k, 128)
            p0[color, rows, :] = (part[color, rows, :] + f32(rx0[color, rows, :])).astype(
                jnp.bfloat16
            )

    nears = {}
    for step in (2, 1, 3):
        for color in range(3):
            add_first(color, step)
            nears[color, step] = send(
                p0.at[color, pl.ds(chunk_at(color, step), CHUNK)],
                near.at[color, step - 1],
                send1.at[color, step - 1],
                recv1.at[color, step - 1],
                along(ORDERS[color][0], step),
            )
    flatten(0, 17)
    for color in range(3):
        first[color, 0].wait_recv()

    second = {}
    for color in range(3):
        for step in (1, 2, 3):
            nears[color, step].wait_recv()
        at = chunk_at(color, 0)
        for k in range(0, CHUNK, 96):
            rows = pl.ds(at + k, 96)
            value = part[color, rows, :] + f32(rx0[color, rows, :])
            for step in range(3):
                value += f32(near[color, step, k : k + 96, :])
            for t in range(4):
                p1[color, k // 24 + t] = value[24 * t : 24 * t + 24].astype(jnp.bfloat16)
        for hop in PLANE:
            second[color, hop] = send(
                p1.at[color, plane_at(color, hop)],
                rx2.at[color, hop - 1],
                send2.at[color, hop - 1],
                recv2.at[color, hop - 1],
                in_plane(color, hop),
            )
    flatten(17, 32)
    fourth = {}
    for color in range(3):
        value = f32(p1[color, plane_at(color, 0)])
        for hop in PLANE:
            second[color, hop].wait_recv()
        for hop in range(1, 16):
            value += f32(rx2[color, hop - 1])
        s_all[grp, color] = value.astype(jnp.bfloat16)
        for r in (3, 2, 1):
            fourth[color, r] = send(
                s_all.at[grp, color],
                s_all.at[grp, color],
                send4.at[color, r - 1],
                recv4.at[color, r - 1],
                grp_peer(r),
            )

    for color in range(3):
        for r in (1, 2, 3):
            fourth[color, r].wait_recv()
    for g in range(4):
        block = jnp.concatenate([f32(s_all[g, color]) for color in range(3)], axis=0)
        out_ref[512:584, 128 * g : 128 * g + 128] = block.astype(jnp.bfloat16)
    for copy in started:
        copy.wait_send()


def score_kernel(x_ref, avg_ref, score_ref, final, gathered, products, flat_avg, score_row, sem):
    grp = lax.axis_index("grp")

    def f32(value):
        return value.astype(jnp.float32)

    def dot(a, b, dims=(((1,), (0,)), ((), ()))):
        return lax.dot_general(a, b, dims, preferred_element_type=jnp.float32)

    def matches(shape, row_of, lane_of):
        return jnp.where(row_of(iota(shape, 0)) == lane_of(iota(shape, 1)), 1.0, 0.0)

    def cos_at(k):
        size = jnp.abs(k - 32)
        return jnp.where(size == 32, 63, size)

    def sin_at(k):
        size = jnp.abs(k - 32)
        return jnp.where(size == 0, -1, jnp.where(size == 32, 64, size + 31))

    row = iota((128, 128), 0)
    lane = iota((128, 128), 1)
    ky = 2 * (row & 31) + ((row >> 5) & 1)
    ysel = jnp.where(
        row < 64,
        jnp.where(cos_at(ky) == lane, 1.0, 0.0),
        jnp.where(sin_at(ky) == lane, jnp.where(ky < 32, -1.0, 1.0), 0.0),
    ).astype(jnp.bfloat16)
    kx = lane & 63
    same = (row >> 6) == (lane >> 6)
    xc = jnp.where(same & (cos_at(kx) == (row & 63)), 1.0, 0.0)
    xs = jnp.where(same & (sin_at(kx) == (row & 63)), jnp.where(kx < 32, -1.0, 1.0), 0.0)
    xsel = jnp.concatenate([xc, xs], axis=1).astype(jnp.bfloat16)
    srow, slane = iota((32, 512), 0), iota((32, 512), 1)
    at = (srow & 7) - 1
    spot = jnp.where(
        ((srow >> 3) == (slane >> 7)) & (at >= 0) & (at < 2) & ((slane & 127) == at * 64), 1.0, 0.0
    ).astype(jnp.bfloat16)
    frow, flane = iota((32, 128), 0), iota((32, 128), 1)
    fy = f32(2 * frow + (flane >> 6) - 32)
    fx = f32((flane & 63) - 32)
    filt = jnp.exp(-(fy * fy + fx * fx) / (BAND * BAND / 2.0))
    bits = iota((8, 128), 1) - 65
    weight = jnp.where((bits >= 0) & (bits < 12), f32(1 << jnp.clip(bits, 0, 12)), 0.0)

    y = dot(ysel[:, :72], x_ref[512:584, 0:512]).astype(jnp.bfloat16)
    y = jnp.concatenate([y[:, 128 * g : 128 * g + 128] for g in range(4)], axis=0)
    z = dot(y, xsel)
    extra = jnp.concatenate([x_ref[576:584, 128 * g : 128 * g + 128] for g in range(4)], axis=0)
    side = dot(ysel, extra, (((1,), (1,)), ((), ()))).astype(jnp.bfloat16)
    side = dot(side, spot)
    half = iota((32, 128), 1) < 64
    for g in range(4):
        rc = z[128 * g : 128 * g + 128, :128]
        rs = z[128 * g : 128 * g + 128, 128:]
        sg = side[:, 128 * g : 128 * g + 128]
        members = jnp.sum(f32(x_ref[576:584, 128 * g : 128 * g + 128]) * weight, axis=1, keepdims=True)
        planes = (rc[:64] - rs[64:] + sg[64:], sg[:64] - rc[64:] - rs[:64])
        for j in range(2):
            scale = filt / (members[1 + j : 2 + j] + ridge)
            for p in range(2):
                even, odd = planes[p][:32], planes[p][32:]
                if j == 0:
                    odd = pltpu.roll(odd, 64, 1)
                else:
                    even = pltpu.roll(even, 64, 1)
                value = jnp.where(half, even, odd) * scale
                final[g, j, p] = value
                gathered[pl.ds(256 * p + 2 * g + j, 32, stride=8), :] = f32(
                    value.astype(jnp.bfloat16)
                )
    for t in range(32):
        for j in range(2):
            flat_avg[j, :, 128 * t : 128 * t + 128] = final[grp, j, :, t, :]
    copy = pltpu.make_async_copy(flat_avg, avg_ref, sem.at[0])
    copy.start()

    energy = jnp.zeros((8, 128), jnp.float32)
    inner = jnp.zeros((512, 16), jnp.float32)
    for t in range(0, 32, 2):
        sides = []
        for u in (t, t + 1):
            re = gathered[8 * u : 8 * u + 8, :]
            im = gathered[256 + 8 * u : 264 + 8 * u, :]
            energy += re * re + im * im
            sides.append(jnp.concatenate([re, im], axis=0).astype(jnp.bfloat16))
        inner += dot(
            x_ref[0:512, 128 * t : 128 * t + 256],
            jnp.concatenate(sides, axis=1),
            (((1,), (1,)), ((), ())),
        )
    products[:, 0:16] = inner
    both = products[pl.ds(0, 256, stride=2), :] + pltpu.roll(
        products[pl.ds(1, 256, stride=2), :], 120, 1
    )
    energy = jnp.sum(energy, axis=1, keepdims=True)
    score_row[...] = (both.T[:8] - 0.5 * energy) / BAND
    last = pltpu.make_async_copy(score_row, score_ref, sem.at[1])
    last.start()
    copy.wait()
    last.wait()


def scores_of(x):
    return pl.pallas_call(
        score_kernel,
        out_shape=(
            jax.ShapeDtypeStruct((2, 2, BAND * BAND), jnp.float32),
            jax.ShapeDtypeStruct((8, 256), jnp.float32),
        ),
        in_specs=[pl.BlockSpec(memory_space=pltpu.VMEM)],
        out_specs=(pl.BlockSpec(memory_space=pl.ANY),) * 2,
        scratch_shapes=[
            pltpu.VMEM((4, 2, 2, 32, 128), jnp.float32),
            pltpu.VMEM((512, 128), jnp.float32),
            pltpu.VMEM((512, 128), jnp.float32),
            pltpu.VMEM((2, 2, BAND * BAND), jnp.float32),
            pltpu.VMEM((8, 256), jnp.float32),
            pltpu.SemaphoreType.DMA((2,)),
        ],
        compiler_params=pltpu.CompilerParams(vmem_limit_bytes=8 << 20),
        name="scores_of",
    )(x)


def reduce_classes(acc, meta, next_block):
    vmem = pl.BlockSpec(memory_space=pltpu.VMEM)
    bf16 = jnp.bfloat16
    return pl.pallas_call(
        reduce_kernel,
        out_shape=pltpu.VMEM((592, 4096), bf16),
        in_specs=[vmem] * 3,
        out_specs=vmem,
        scratch_shapes=[
            pltpu.VMEM((64, PIX, 128), bf16),
            pltpu.VMEM((PIX, 128), jnp.float32),
            pltpu.VMEM((PIX, 128), jnp.float32),
            pltpu.VMEM((3, 1536, 128), jnp.float32),
            pltpu.VMEM((3, 1536, 128), bf16),
            pltpu.VMEM((3, 1536, 128), bf16),
            pltpu.VMEM((3, 1536, 128), bf16),
            pltpu.VMEM((3, 3, CHUNK, 128), bf16),
            pltpu.VMEM((3, 16, 24, 128), bf16),
            pltpu.VMEM((3, 15, 24, 128), bf16),
            pltpu.VMEM((4, 3, 24, 128), bf16),
            pltpu.VMEM((2 * PIX, 256), bf16),
            pltpu.SemaphoreType.DMA((3, 4)),
            pltpu.SemaphoreType.DMA((3, 4)),
            pltpu.SemaphoreType.DMA((3, 6)),
            pltpu.SemaphoreType.DMA((3, 6)),
            pltpu.SemaphoreType.DMA((3, 15)),
            pltpu.SemaphoreType.DMA((3, 15)),
            pltpu.SemaphoreType.DMA((3, 3)),
            pltpu.SemaphoreType.DMA((3, 3)),
        ],
        compiler_params=pltpu.CompilerParams(
            collective_id=0, has_side_effects=True, vmem_limit_bytes=24 << 20
        ),
        name="reduce_classes",
    )(acc, meta, next_block)


def body(images, shifts, class_ids, next_block):
    meta = jnp.concatenate([shifts.T, class_ids[None, :]], axis=0)
    return tuple(scores_of(reduce_classes(class_images(images, meta), meta, next_block)))


def solution(mesh):
    placed = (
        P(("dp", "grp"), None, None),
        P(("dp", "grp"), None),
        P(("dp", "grp")),
        P("grp", None, None),
    )
    return jax.shard_map(
        body,
        mesh=mesh,
        in_specs=placed,
        out_specs=(P(("dp", "grp"), None, None), P("dp", "grp")),
        check_vma=False,
    )
```

```python
import math

import jax
import jax.numpy as jnp
from jax import lax
from jax.experimental import pallas as pl
from jax.experimental.pallas import tpu as pltpu
from jax.sharding import PartitionSpec as P

PIX = 128
BAND = 64
CLASSES = 256
REACH = 16
ROWS = PIX + 2 * REACH
OUT_ROWS = 72
STEP = 32
GROUP = 64
BATCH = 32
ridge = 4.0


def iota(shape, axis):
    return lax.broadcasted_iota(jnp.int32, shape, axis)


def wave(position, b):
    is_sin = ((b >= 32) & (b < 63)) | (b == 64)
    freq = jnp.where(b < 32, b, jnp.where(b < 63, b - 31, 32))
    residue = (position * freq - jnp.where(is_sin, 32, 0)) & (PIX - 1)
    value = jnp.cos(residue.astype(jnp.float32) * (2.0 * math.pi / PIX))
    return jnp.where(b <= 64, value * (1.0 / math.sqrt(PIX)), 0.0)


def class_kernel(meta_ref, img_hbm, acc, imgs, packed, codes, img_sem, code_sem):
    count = imgs.shape[0]

    def chunk(k):
        at = pl.ds(k * STEP, STEP)
        return pltpu.make_async_copy(img_hbm.at[at], imgs.at[at], img_sem.at[k])

    for k in range(count // STEP):
        chunk(k).start()

    packed[...] = (meta_ref[2:3, :] * 64 + meta_ref[1:2, :] + REACH) * PIX + (
        meta_ref[0:1, :] & (PIX - 1)
    )
    code_copy = pltpu.make_async_copy(packed, codes, code_sem.at[0])
    code_copy.start()
    flat = wave(iota((PIX, 128), 0), iota((PIX, 128), 1))
    acc[CLASSES, 0:PIX, :] = flat
    acc[CLASSES + 1, 0:OUT_ROWS, :] = wave(iota((OUT_ROWS, PIX), 1), iota((OUT_ROWS, PIX), 0))
    lane = iota((PIX, 128), 1)
    low = jnp.where(lane < 64, flat, 0.0)
    turn = iota((PIX, 128), 0) & 3
    last = jnp.where(turn == 1, 1.0, jnp.where(turn == 3, -1.0, 0.0)) * (1.0 / math.sqrt(PIX))
    for j in range(2):
        acc[CLASSES + 2 + j, 0:PIX, :] = pltpu.roll(low, 64 * j, 1)
        acc[CLASSES + 4 + j, 0:PIX, :] = jnp.where(lane % 2 == j, last, 0.0)

    def clear(c, carry):
        acc[c] = jnp.zeros((ROWS, PIX), jnp.float32)
        return carry

    lax.fori_loop(0, CLASSES, clear, 0, unroll=4)

    def add_chunk(k, carry):
        for n in range(GROUP // STEP):
            chunk(k * (GROUP // STEP) + n).wait()

        def add_image(n, inner):
            i = k * GROUP + n
            code = codes[0, i]
            moved = pltpu.roll(imgs[i].astype(jnp.float32), code & (PIX - 1), 1)
            acc[code >> 13, pl.ds((code >> 7) & 63, PIX), :] += moved
            return inner

        return lax.fori_loop(0, GROUP, add_image, carry, unroll=GROUP)

    code_copy.wait()
    lax.fori_loop(0, count // GROUP, add_chunk, 0)


def class_images(images, meta):
    return pl.pallas_call(
        class_kernel,
        out_shape=pltpu.VMEM((CLASSES + 6, ROWS, PIX), jnp.float32),
        in_specs=[
            pl.BlockSpec(memory_space=pltpu.VMEM),
            pl.BlockSpec(memory_space=pl.ANY),
        ],
        out_specs=pl.BlockSpec(memory_space=pltpu.VMEM),
        scratch_shapes=[
            pltpu.VMEM(images.shape, jnp.bfloat16),
            pltpu.VMEM((1, images.shape[0]), jnp.int32),
            pltpu.SMEM((1, images.shape[0]), jnp.int32),
            pltpu.SemaphoreType.DMA((images.shape[0] // STEP,)),
            pltpu.SemaphoreType.DMA((1,)),
        ],
        compiler_params=pltpu.CompilerParams(vmem_limit_bytes=20 << 20),
        name="class_images",
    )(meta, images)


PLANE = (10, 9, 11, 6, 14, 8, 2, 5, 7, 13, 15, 4, 12, 1, 3)
ORDERS = ((0, 1, 2), (1, 2, 0), (2, 0, 1))
CHUNK = 384
HALF = 192
MESH_ID = pl.DeviceIdType.MESH


def reduce_kernel(
    acc,
    meta_ref,
    next_ref,
    out_ref,
    x2,
    edge,
    side_rows,
    part,
    outgoing,
    rx0,
    p0,
    near,
    p1,
    rx2,
    s_all,
    w1_ref,
    send0,
    recv0,
    send1,
    recv1,
    send2,
    recv2,
    send4,
    recv4,
):
    dp = lax.axis_index("dp")
    grp = lax.axis_index("grp")
    core = grp % 2
    here = (dp // 8, (grp // 2) * 2 + (dp // 4) % 2, dp % 4)

    def device(spot, on_core):
        x, y, z = spot
        return {"dp": (x * 2 + y % 2) * 4 + z, "grp": (y // 2) * 2 + on_core}

    def along(dim, step):
        spot = list(here)
        spot[dim] = (spot[dim] + step) % 4
        return device(spot, core)

    def in_plane(color, hop):
        _, one, two = ORDERS[color]
        spot = list(here)
        spot[one] = (spot[one] + hop // 4) % 4
        spot[two] = (spot[two] + hop % 4) % 4
        return device(spot, core)

    def plane_at(color, hop):
        _, one, two = ORDERS[color]
        return (here[one] + hop // 4) % 4 * 4 + (here[two] + hop % 4) % 4

    partner = {"dp": dp, "grp": grp + 1 - 2 * core}

    def grp_peer(r):
        low = (grp % 2 + r % 2) % 2
        high = (grp // 2 + r // 2) % 2
        return {"dp": dp, "grp": high * 2 + low}

    def flatten(lo, hi):
        def one(g, carry):
            block = next_ref[pl.ds(g * 8, 8)]
            out_ref[pl.ds(pl.multiple_of(g * 16, 16), 16), :] = block.reshape(16, block.shape[2])
            return carry

        lax.fori_loop(lo, hi, one, 0)

    barrier = pltpu.get_barrier_semaphore()
    peers = [partner, grp_peer(3)] + [along(d, s) for d in range(3) for s in (1, 2, 3)]
    peers += [in_plane(c, h) for c in range(3) for h in range(1, 16) if h // 4 and h % 4]
    for peer in peers:
        pl.semaphore_signal(barrier, inc=1, device_id=peer, device_id_type=MESH_ID)
    started = []

    def send(src, dst, ssem, rsem, where):
        copy = pltpu.make_async_remote_copy(
            src_ref=src,
            dst_ref=dst,
            send_sem=ssem,
            recv_sem=rsem,
            device_id=where,
            device_id_type=MESH_ID,
        )
        copy.start()
        started.append(copy)
        return copy

    def chunk_at(color, step):
        return pl.multiple_of(((here[ORDERS[color][0]] + step) % 4) * CHUNK, CHUNK)

    lane128 = iota((PIX, 128), 1)
    byc = acc[CLASSES, 0:PIX, :].astype(jnp.bfloat16)
    byr = acc[CLASSES + 1, 0:OUT_ROWS, :].astype(jnp.bfloat16)
    for j in range(2):
        for h in range(2):
            w1_ref[PIX * j : PIX * j + PIX, 128 * h : 128 * h + 128] = acc[
                CLASSES + 2 + 2 * h + j, 0:PIX, :
            ].astype(jnp.bfloat16)
    lane_pair = lane128 // 2

    def folded(c):
        return jnp.concatenate(
            [
                acc[c, 16:32, :] + acc[c, 144:160, :],
                acc[c, 32:128, :],
                acc[c, 128:144, :] + acc[c, 0:16, :],
            ],
            axis=0,
        ).astype(jnp.bfloat16)

    def transform(on_core):
        def columns_of(p, carry):
            chip = p * BATCH
            lhs = []
            for k in range(BATCH):
                c = (chip + k) * 4 + 2 * on_core
                lhs.append(jnp.concatenate([folded(c), folded(c + 1)], axis=1))
            got = jnp.dot(
                jnp.concatenate(lhs, axis=0), w1_ref[...], preferred_element_type=jnp.float32
            )
            for k in range(BATCH):
                mine = got[PIX * k : PIX * k + PIX]
                x2[chip + k] = mine[:, :128].astype(jnp.bfloat16)
                pltpu.store(edge, mine[:, 128:], mask=lane_pair == chip + k)
            return carry

        lax.fori_loop(0, 64 // BATCH, columns_of, 0)
        side = lax.dot_general(
            edge[...].astype(jnp.bfloat16),
            byc,
            (((0,), (0,)), ((), ())),
            preferred_element_type=jnp.float32,
        )
        row = iota((128, meta_ref.shape[1]), 0)
        cls = (row // 2) * 4 + 2 * on_core + row % 2
        tally = jnp.sum(
            jnp.where(cls == meta_ref[2:3, :], 1.0, 0.0), axis=1, keepdims=True
        ).astype(jnp.int32)
        bit = lane128 - 65
        tally = jnp.where((bit >= 0) & (bit < 12), (tally >> jnp.clip(bit, 0, 12)) & 1, 0)
        side_rows[...] = side + tally.astype(jnp.float32)

        def rows_of(m, carry):
            eight = side_rows[pl.ds(pl.multiple_of(m * 8, 8), 8), :]
            sub = iota((8, 128), 0)
            place = (sub == 1) | (sub == 2)
            for k in range(0, 4, 2):
                q = m * 4 + k
                got = jnp.dot(
                    byr,
                    jnp.concatenate([x2[q], x2[q + 1]], axis=1),
                    preferred_element_type=jnp.float32,
                )
                for n in range(2):
                    q = m * 4 + k + n
                    block = got[:, 128 * n : 128 * n + 128]
                    extra = jnp.where(place, pltpu.roll(eight, (1 - 2 * (k + n)) % 8, 0), 0.0)
                    block = jnp.concatenate([block[:64], block[64:] + extra], axis=0)
                    x, y, z = q // 16, (q % 2) * 2 + (q // 8) % 2, (q // 2) % 4
                    spots = (x * 16 + y * 4 + z, y * 16 + z * 4 + x, z * 16 + x * 4 + y)
                    for color in range(3):
                        at = pl.multiple_of(spots[color] * 24, 8)
                        part[color, pl.ds(at, 24), :] = block[24 * color : 24 * color + 24]
            return carry

        lax.fori_loop(0, 16, rows_of, 0, unroll=16)

    transform(1 - core)
    first = {}
    for step in (2, 1, 3, 0):
        for color in range(3):
            at = chunk_at(color, step)
            for k in range(0, CHUNK, 128):
                rows = pl.ds(at + k, 128)
                outgoing[color, rows, :] = part[color, rows, :].astype(jnp.bfloat16)
    pl.semaphore_wait(barrier, len(peers))
    for step in (2, 1, 3, 0):
        for color in range(3):
            at = chunk_at(color, step)
            first[color, step] = send(
                outgoing.at[color, pl.ds(at, CHUNK)],
                rx0.at[color, pl.ds(at, CHUNK)],
                send0.at[color, step],
                recv0.at[color, step],
                partner,
            )
    transform(core)

    def f32(value):
        return value.astype(jnp.float32)

    def add_first(color, step):
        first[color, step].wait_recv()
        at = chunk_at(color, step)
        for k in range(0, CHUNK, 128):
            rows = pl.ds(at + k, 128)
            p0[color, rows, :] = (part[color, rows, :] + f32(rx0[color, rows, :])).astype(
                jnp.bfloat16
            )

    nears = {}
    for step in (2, 1, 3):
        for color in range(3):
            add_first(color, step)
            nears[color, step] = send(
                p0.at[color, pl.ds(chunk_at(color, step), CHUNK)],
                near.at[color, step - 1],
                send1.at[color, step - 1],
                recv1.at[color, step - 1],
                along(ORDERS[color][0], step),
            )
    flatten(0, 17)
    for color in range(3):
        first[color, 0].wait_recv()

    second = {}
    for color in range(3):
        for step in (1, 2, 3):
            nears[color, step].wait_recv()
        at = chunk_at(color, 0)
        for k in range(0, CHUNK, 96):
            rows = pl.ds(at + k, 96)
            value = part[color, rows, :] + f32(rx0[color, rows, :])
            for step in range(3):
                value += f32(near[color, step, k : k + 96, :])
            for t in range(4):
                p1[color, k // 24 + t] = value[24 * t : 24 * t + 24].astype(jnp.bfloat16)
        for hop in PLANE:
            second[color, hop] = send(
                p1.at[color, plane_at(color, hop)],
                rx2.at[color, hop - 1],
                send2.at[color, hop - 1],
                recv2.at[color, hop - 1],
                in_plane(color, hop),
            )
    flatten(17, 32)
    fourth = {}
    for color in range(3):
        value = f32(p1[color, plane_at(color, 0)])
        for hop in PLANE:
            second[color, hop].wait_recv()
        for hop in range(1, 16):
            value += f32(rx2[color, hop - 1])
        s_all[grp, color] = value.astype(jnp.bfloat16)
        for r in (3, 2, 1):
            fourth[color, r] = send(
                s_all.at[grp, color],
                s_all.at[grp, color],
                send4.at[color, r - 1],
                recv4.at[color, r - 1],
                grp_peer(r),
            )

    for color in range(3):
        for r in (1, 2, 3):
            fourth[color, r].wait_recv()
    for g in range(4):
        block = jnp.concatenate([f32(s_all[g, color]) for color in range(3)], axis=0)
        out_ref[512:584, 128 * g : 128 * g + 128] = block.astype(jnp.bfloat16)
    for copy in started:
        copy.wait_send()


def score_kernel(x_ref, avg_ref, score_ref, final, gathered, products, flat_avg, score_row, sem):
    grp = lax.axis_index("grp")

    def f32(value):
        return value.astype(jnp.float32)

    def dot(a, b, dims=(((1,), (0,)), ((), ()))):
        return lax.dot_general(a, b, dims, preferred_element_type=jnp.float32)

    def matches(shape, row_of, lane_of):
        return jnp.where(row_of(iota(shape, 0)) == lane_of(iota(shape, 1)), 1.0, 0.0)

    def cos_at(k):
        size = jnp.abs(k - 32)
        return jnp.where(size == 32, 63, size)

    def sin_at(k):
        size = jnp.abs(k - 32)
        return jnp.where(size == 0, -1, jnp.where(size == 32, 64, size + 31))

    row = iota((128, 128), 0)
    lane = iota((128, 128), 1)
    ky = 2 * (row & 31) + ((row >> 5) & 1)
    ysel = jnp.where(
        row < 64,
        jnp.where(cos_at(ky) == lane, 1.0, 0.0),
        jnp.where(sin_at(ky) == lane, jnp.where(ky < 32, -1.0, 1.0), 0.0),
    ).astype(jnp.bfloat16)
    kx = lane & 63
    same = (row >> 6) == (lane >> 6)
    xc = jnp.where(same & (cos_at(kx) == (row & 63)), 1.0, 0.0)
    xs = jnp.where(same & (sin_at(kx) == (row & 63)), jnp.where(kx < 32, -1.0, 1.0), 0.0)
    xsel = jnp.concatenate([xc, xs], axis=1).astype(jnp.bfloat16)
    srow, slane = iota((32, 512), 0), iota((32, 512), 1)
    at = (srow & 7) - 1
    spot = jnp.where(
        ((srow >> 3) == (slane >> 7)) & (at >= 0) & (at < 2) & ((slane & 127) == at * 64), 1.0, 0.0
    ).astype(jnp.bfloat16)
    frow, flane = iota((32, 128), 0), iota((32, 128), 1)
    fy = f32(2 * frow + (flane >> 6) - 32)
    fx = f32((flane & 63) - 32)
    filt = jnp.exp(-(fy * fy + fx * fx) / (BAND * BAND / 2.0))
    bits = iota((8, 128), 1) - 65
    weight = jnp.where((bits >= 0) & (bits < 12), f32(1 << jnp.clip(bits, 0, 12)), 0.0)

    y = dot(ysel[:, :72], x_ref[512:584, 0:512]).astype(jnp.bfloat16)
    y = jnp.concatenate([y[:, 128 * g : 128 * g + 128] for g in range(4)], axis=0)
    z = dot(y, xsel)
    extra = jnp.concatenate([x_ref[576:584, 128 * g : 128 * g + 128] for g in range(4)], axis=0)
    side = dot(ysel, extra, (((1,), (1,)), ((), ()))).astype(jnp.bfloat16)
    side = dot(side, spot)
    half = iota((32, 128), 1) < 64
    for g in range(4):
        rc = z[128 * g : 128 * g + 128, :128]
        rs = z[128 * g : 128 * g + 128, 128:]
        sg = side[:, 128 * g : 128 * g + 128]
        members = jnp.sum(f32(x_ref[576:584, 128 * g : 128 * g + 128]) * weight, axis=1, keepdims=True)
        planes = (rc[:64] - rs[64:] + sg[64:], sg[:64] - rc[64:] - rs[:64])
        for j in range(2):
            scale = filt / (members[1 + j : 2 + j] + ridge)
            for p in range(2):
                even, odd = planes[p][:32], planes[p][32:]
                if j == 0:
                    odd = pltpu.roll(odd, 64, 1)
                else:
                    even = pltpu.roll(even, 64, 1)
                value = jnp.where(half, even, odd) * scale
                final[g, j, p] = value
                gathered[pl.ds(256 * p + 2 * g + j, 32, stride=8), :] = f32(
                    value.astype(jnp.bfloat16)
                )
    for t in range(32):
        for j in range(2):
            flat_avg[j, :, 128 * t : 128 * t + 128] = final[grp, j, :, t, :]
    copy = pltpu.make_async_copy(flat_avg, avg_ref, sem.at[0])
    copy.start()

    energy = jnp.zeros((8, 128), jnp.float32)
    inner = jnp.zeros((512, 16), jnp.float32)
    for t in range(0, 32, 2):
        sides = []
        for u in (t, t + 1):
            re = gathered[8 * u : 8 * u + 8, :]
            im = gathered[256 + 8 * u : 264 + 8 * u, :]
            energy += re * re + im * im
            sides.append(jnp.concatenate([re, im], axis=0).astype(jnp.bfloat16))
        inner += dot(
            x_ref[0:512, 128 * t : 128 * t + 256],
            jnp.concatenate(sides, axis=1),
            (((1,), (1,)), ((), ())),
        )
    products[:, 0:16] = inner
    both = products[pl.ds(0, 256, stride=2), :] + pltpu.roll(
        products[pl.ds(1, 256, stride=2), :], 120, 1
    )
    energy = jnp.sum(energy, axis=1, keepdims=True)
    score_row[...] = (both.T[:8] - 0.5 * energy) / BAND
    last = pltpu.make_async_copy(score_row, score_ref, sem.at[1])
    last.start()
    copy.wait()
    last.wait()


def scores_of(x):
    return pl.pallas_call(
        score_kernel,
        out_shape=(
            jax.ShapeDtypeStruct((2, 2, BAND * BAND), jnp.float32),
            jax.ShapeDtypeStruct((8, 256), jnp.float32),
        ),
        in_specs=[pl.BlockSpec(memory_space=pltpu.VMEM)],
        out_specs=(pl.BlockSpec(memory_space=pl.ANY),) * 2,
        scratch_shapes=[
            pltpu.VMEM((4, 2, 2, 32, 128), jnp.float32),
            pltpu.VMEM((512, 128), jnp.float32),
            pltpu.VMEM((512, 128), jnp.float32),
            pltpu.VMEM((2, 2, BAND * BAND), jnp.float32),
            pltpu.VMEM((8, 256), jnp.float32),
            pltpu.SemaphoreType.DMA((2,)),
        ],
        compiler_params=pltpu.CompilerParams(vmem_limit_bytes=8 << 20),
        name="scores_of",
    )(x)


def reduce_classes(acc, meta, next_block):
    vmem = pl.BlockSpec(memory_space=pltpu.VMEM)
    bf16 = jnp.bfloat16
    return pl.pallas_call(
        reduce_kernel,
        out_shape=pltpu.VMEM((592, 4096), bf16),
        in_specs=[vmem] * 3,
        out_specs=vmem,
        scratch_shapes=[
            pltpu.VMEM((64, PIX, 128), bf16),
            pltpu.VMEM((PIX, 128), jnp.float32),
            pltpu.VMEM((PIX, 128), jnp.float32),
            pltpu.VMEM((3, 1536, 128), jnp.float32),
            pltpu.VMEM((3, 1536, 128), bf16),
            pltpu.VMEM((3, 1536, 128), bf16),
            pltpu.VMEM((3, 1536, 128), bf16),
            pltpu.VMEM((3, 3, CHUNK, 128), bf16),
            pltpu.VMEM((3, 16, 24, 128), bf16),
            pltpu.VMEM((3, 15, 24, 128), bf16),
            pltpu.VMEM((4, 3, 24, 128), bf16),
            pltpu.VMEM((2 * PIX, 256), bf16),
            pltpu.SemaphoreType.DMA((3, 4)),
            pltpu.SemaphoreType.DMA((3, 4)),
            pltpu.SemaphoreType.DMA((3, 6)),
            pltpu.SemaphoreType.DMA((3, 6)),
            pltpu.SemaphoreType.DMA((3, 15)),
            pltpu.SemaphoreType.DMA((3, 15)),
            pltpu.SemaphoreType.DMA((3, 3)),
            pltpu.SemaphoreType.DMA((3, 3)),
        ],
        compiler_params=pltpu.CompilerParams(
            collective_id=0, has_side_effects=True, vmem_limit_bytes=24 << 20
        ),
        name="reduce_classes",
    )(acc, meta, next_block)


def body(images, shifts, class_ids, next_block):
    meta = jnp.concatenate([shifts.T, class_ids[None, :]], axis=0)
    return tuple(scores_of(reduce_classes(class_images(images, meta), meta, next_block)))


def solution(mesh):
    placed = (
        P(("dp", "grp"), None, None),
        P(("dp", "grp"), None),
        P(("dp", "grp")),
        P("grp", None, None),
    )
    return jax.shard_map(
        body,
        mesh=mesh,
        in_specs=placed,
        out_specs=(P(("dp", "grp"), None, None), P("dp", "grp")),
        check_vma=False,
    )
```

```python
import math

import jax
import jax.numpy as jnp
from jax import lax
from jax.experimental import pallas as pl
from jax.experimental.pallas import tpu as pltpu
from jax.sharding import PartitionSpec as P

PIX = 128
BAND = 64
CLASSES = 256
REACH = 16
ROWS = PIX + 2 * REACH
OUT_ROWS = 72
STEP = 32
GROUP = 64
BATCH = 32
ridge = 4.0


def iota(shape, axis):
    return lax.broadcasted_iota(jnp.int32, shape, axis)


def wave(position, b):
    is_sin = ((b >= 32) & (b < 63)) | (b == 64)
    freq = jnp.where(b < 32, b, jnp.where(b < 63, b - 31, 32))
    residue = (position * freq - jnp.where(is_sin, 32, 0)) & (PIX - 1)
    value = jnp.cos(residue.astype(jnp.float32) * (2.0 * math.pi / PIX))
    return jnp.where(b <= 64, value * (1.0 / math.sqrt(PIX)), 0.0)


def class_kernel(meta_ref, img_hbm, acc, imgs, packed, codes, img_sem, code_sem):
    count = imgs.shape[0]

    def chunk(k):
        at = pl.ds(k * STEP, STEP)
        return pltpu.make_async_copy(img_hbm.at[at], imgs.at[at], img_sem.at[k])

    for k in range(count // STEP):
        chunk(k).start()

    packed[...] = (meta_ref[2:3, :] * 64 + meta_ref[1:2, :] + REACH) * PIX + (
        meta_ref[0:1, :] & (PIX - 1)
    )
    code_copy = pltpu.make_async_copy(packed, codes, code_sem.at[0])
    code_copy.start()
    flat = wave(iota((PIX, 128), 0), iota((PIX, 128), 1))
    acc[CLASSES, 0:PIX, :] = flat
    acc[CLASSES + 1, 0:OUT_ROWS, :] = wave(iota((OUT_ROWS, PIX), 1), iota((OUT_ROWS, PIX), 0))
    lane = iota((PIX, 128), 1)
    low = jnp.where(lane < 64, flat, 0.0)
    turn = iota((PIX, 128), 0) & 3
    last = jnp.where(turn == 1, 1.0, jnp.where(turn == 3, -1.0, 0.0)) * (1.0 / math.sqrt(PIX))
    for j in range(2):
        acc[CLASSES + 2 + j, 0:PIX, :] = pltpu.roll(low, 64 * j, 1)
        acc[CLASSES + 4 + j, 0:PIX, :] = jnp.where(lane % 2 == j, last, 0.0)

    def clear(c, carry):
        acc[c] = jnp.zeros((ROWS, PIX), jnp.float32)
        return carry

    lax.fori_loop(0, CLASSES, clear, 0, unroll=4)

    def add_chunk(k, carry):
        for n in range(GROUP // STEP):
            chunk(k * (GROUP // STEP) + n).wait()

        def add_image(n, inner):
            i = k * GROUP + n
            code = codes[0, i]
            moved = pltpu.roll(imgs[i].astype(jnp.float32), code & (PIX - 1), 1)
            acc[code >> 13, pl.ds((code >> 7) & 63, PIX), :] += moved
            return inner

        return lax.fori_loop(0, GROUP, add_image, carry, unroll=GROUP)

    code_copy.wait()
    lax.fori_loop(0, count // GROUP, add_chunk, 0)


def class_images(images, meta):
    return pl.pallas_call(
        class_kernel,
        out_shape=pltpu.VMEM((CLASSES + 6, ROWS, PIX), jnp.float32),
        in_specs=[
            pl.BlockSpec(memory_space=pltpu.VMEM),
            pl.BlockSpec(memory_space=pl.ANY),
        ],
        out_specs=pl.BlockSpec(memory_space=pltpu.VMEM),
        scratch_shapes=[
            pltpu.VMEM(images.shape, jnp.bfloat16),
            pltpu.VMEM((1, images.shape[0]), jnp.int32),
            pltpu.SMEM((1, images.shape[0]), jnp.int32),
            pltpu.SemaphoreType.DMA((images.shape[0] // STEP,)),
            pltpu.SemaphoreType.DMA((1,)),
        ],
        compiler_params=pltpu.CompilerParams(vmem_limit_bytes=20 << 20),
        name="class_images",
    )(meta, images)


PLANE = (10, 9, 11, 6, 14, 8, 2, 5, 7, 13, 15, 4, 12, 1, 3)
ORDERS = ((0, 1, 2), (1, 2, 0), (2, 0, 1))
CHUNK = 384
HALF = 192
MESH_ID = pl.DeviceIdType.MESH


def reduce_kernel(
    acc,
    meta_ref,
    next_ref,
    out_ref,
    x2,
    edge,
    side_rows,
    part,
    outgoing,
    rx0,
    p0,
    near,
    p1,
    rx2,
    s_all,
    w1_ref,
    send0,
    recv0,
    send1,
    recv1,
    send2,
    recv2,
    send4,
    recv4,
):
    dp = lax.axis_index("dp")
    grp = lax.axis_index("grp")
    core = grp % 2
    here = (dp // 8, (grp // 2) * 2 + (dp // 4) % 2, dp % 4)

    def device(spot, on_core):
        x, y, z = spot
        return {"dp": (x * 2 + y % 2) * 4 + z, "grp": (y // 2) * 2 + on_core}

    def along(dim, step):
        spot = list(here)
        spot[dim] = (spot[dim] + step) % 4
        return device(spot, core)

    def in_plane(color, hop):
        _, one, two = ORDERS[color]
        spot = list(here)
        spot[one] = (spot[one] + hop // 4) % 4
        spot[two] = (spot[two] + hop % 4) % 4
        return device(spot, core)

    def plane_at(color, hop):
        _, one, two = ORDERS[color]
        return (here[one] + hop // 4) % 4 * 4 + (here[two] + hop % 4) % 4

    partner = {"dp": dp, "grp": grp + 1 - 2 * core}

    def grp_peer(r):
        low = (grp % 2 + r % 2) % 2
        high = (grp // 2 + r // 2) % 2
        return {"dp": dp, "grp": high * 2 + low}

    def flatten(lo, hi):
        def one(g, carry):
            block = next_ref[pl.ds(g * 8, 8)]
            out_ref[pl.ds(pl.multiple_of(g * 16, 16), 16), :] = block.reshape(16, block.shape[2])
            return carry

        lax.fori_loop(lo, hi, one, 0)

    barrier = pltpu.get_barrier_semaphore()
    peers = [partner, grp_peer(3)] + [along(d, s) for d in range(3) for s in (1, 2, 3)]
    peers += [in_plane(c, h) for c in range(3) for h in range(1, 16) if h // 4 and h % 4]
    for peer in peers:
        pl.semaphore_signal(barrier, inc=1, device_id=peer, device_id_type=MESH_ID)
    started = []

    def send(src, dst, ssem, rsem, where):
        copy = pltpu.make_async_remote_copy(
            src_ref=src,
            dst_ref=dst,
            send_sem=ssem,
            recv_sem=rsem,
            device_id=where,
            device_id_type=MESH_ID,
        )
        copy.start()
        started.append(copy)
        return copy

    def chunk_at(color, step):
        return pl.multiple_of(((here[ORDERS[color][0]] + step) % 4) * CHUNK, CHUNK)

    lane128 = iota((PIX, 128), 1)
    byc = acc[CLASSES, 0:PIX, :].astype(jnp.bfloat16)
    byr = acc[CLASSES + 1, 0:OUT_ROWS, :].astype(jnp.bfloat16)
    for j in range(2):
        for h in range(2):
            w1_ref[PIX * j : PIX * j + PIX, 128 * h : 128 * h + 128] = acc[
                CLASSES + 2 + 2 * h + j, 0:PIX, :
            ].astype(jnp.bfloat16)
    lane_pair = lane128 // 2

    def folded(c):
        return jnp.concatenate(
            [
                acc[c, 16:32, :] + acc[c, 144:160, :],
                acc[c, 32:128, :],
                acc[c, 128:144, :] + acc[c, 0:16, :],
            ],
            axis=0,
        ).astype(jnp.bfloat16)

    def transform(on_core):
        def columns_of(p, carry):
            chip = p * BATCH
            lhs = []
            for k in range(BATCH):
                c = (chip + k) * 4 + 2 * on_core
                lhs.append(jnp.concatenate([folded(c), folded(c + 1)], axis=1))
            got = jnp.dot(
                jnp.concatenate(lhs, axis=0), w1_ref[...], preferred_element_type=jnp.float32
            )
            for k in range(BATCH):
                mine = got[PIX * k : PIX * k + PIX]
                x2[chip + k] = mine[:, :128].astype(jnp.bfloat16)
                pltpu.store(edge, mine[:, 128:], mask=lane_pair == chip + k)
            return carry

        lax.fori_loop(0, 64 // BATCH, columns_of, 0)
        side = lax.dot_general(
            edge[...].astype(jnp.bfloat16),
            byc,
            (((0,), (0,)), ((), ())),
            preferred_element_type=jnp.float32,
        )
        row = iota((128, meta_ref.shape[1]), 0)
        cls = (row // 2) * 4 + 2 * on_core + row % 2
        tally = jnp.sum(
            jnp.where(cls == meta_ref[2:3, :], 1.0, 0.0), axis=1, keepdims=True
        ).astype(jnp.int32)
        bit = lane128 - 65
        tally = jnp.where((bit >= 0) & (bit < 12), (tally >> jnp.clip(bit, 0, 12)) & 1, 0)
        side_rows[...] = side + tally.astype(jnp.float32)

        def rows_of(m, carry):
            eight = side_rows[pl.ds(pl.multiple_of(m * 8, 8), 8), :]
            sub = iota((8, 128), 0)
            place = (sub == 1) | (sub == 2)
            for k in range(0, 4, 2):
                q = m * 4 + k
                got = jnp.dot(
                    byr,
                    jnp.concatenate([x2[q], x2[q + 1]], axis=1),
                    preferred_element_type=jnp.float32,
                )
                for n in range(2):
                    q = m * 4 + k + n
                    block = got[:, 128 * n : 128 * n + 128]
                    extra = jnp.where(place, pltpu.roll(eight, (1 - 2 * (k + n)) % 8, 0), 0.0)
                    block = jnp.concatenate([block[:64], block[64:] + extra], axis=0)
                    x, y, z = q // 16, (q % 2) * 2 + (q // 8) % 2, (q // 2) % 4
                    spots = (x * 16 + y * 4 + z, y * 16 + z * 4 + x, z * 16 + x * 4 + y)
                    for color in range(3):
                        at = pl.multiple_of(spots[color] * 24, 8)
                        part[color, pl.ds(at, 24), :] = block[24 * color : 24 * color + 24]
            return carry

        lax.fori_loop(0, 16, rows_of, 0, unroll=16)

    transform(1 - core)
    first = {}
    for step in (2, 1, 3, 0):
        for color in range(3):
            at = chunk_at(color, step)
            for k in range(0, CHUNK, 128):
                rows = pl.ds(at + k, 128)
                outgoing[color, rows, :] = part[color, rows, :].astype(jnp.bfloat16)
    pl.semaphore_wait(barrier, len(peers))
    for step in (2, 1, 3, 0):
        for color in range(3):
            at = chunk_at(color, step)
            first[color, step] = send(
                outgoing.at[color, pl.ds(at, CHUNK)],
                rx0.at[color, pl.ds(at, CHUNK)],
                send0.at[color, step],
                recv0.at[color, step],
                partner,
            )
    transform(core)

    def f32(value):
        return value.astype(jnp.float32)

    def add_first(color, step):
        first[color, step].wait_recv()
        at = chunk_at(color, step)
        for k in range(0, CHUNK, 128):
            rows = pl.ds(at + k, 128)
            p0[color, rows, :] = (part[color, rows, :] + f32(rx0[color, rows, :])).astype(
                jnp.bfloat16
            )

    nears = {}
    for step in (2, 1, 3):
        for color in range(3):
            add_first(color, step)
            nears[color, step] = send(
                p0.at[color, pl.ds(chunk_at(color, step), CHUNK)],
                near.at[color, step - 1],
                send1.at[color, step - 1],
                recv1.at[color, step - 1],
                along(ORDERS[color][0], step),
            )
    flatten(0, 17)
    for color in range(3):
        first[color, 0].wait_recv()

    second = {}
    for color in range(3):
        for step in (1, 2, 3):
            nears[color, step].wait_recv()
        at = chunk_at(color, 0)
        for k in range(0, CHUNK, 96):
            rows = pl.ds(at + k, 96)
            value = part[color, rows, :] + f32(rx0[color, rows, :])
            for step in range(3):
                value += f32(near[color, step, k : k + 96, :])
            for t in range(4):
                p1[color, k // 24 + t] = value[24 * t : 24 * t + 24].astype(jnp.bfloat16)
        for hop in PLANE:
            second[color, hop] = send(
                p1.at[color, plane_at(color, hop)],
                rx2.at[color, hop - 1],
                send2.at[color, hop - 1],
                recv2.at[color, hop - 1],
                in_plane(color, hop),
            )
    flatten(17, 32)
    fourth = {}
    for color in range(3):
        value = f32(p1[color, plane_at(color, 0)])
        for hop in PLANE:
            second[color, hop].wait_recv()
        for hop in range(1, 16):
            value += f32(rx2[color, hop - 1])
        s_all[grp, color] = value.astype(jnp.bfloat16)
        for r in (3, 2, 1):
            fourth[color, r] = send(
                s_all.at[grp, color],
                s_all.at[grp, color],
                send4.at[color, r - 1],
                recv4.at[color, r - 1],
                grp_peer(r),
            )

    for color in range(3):
        for r in (1, 2, 3):
            fourth[color, r].wait_recv()
    for g in range(4):
        block = jnp.concatenate([f32(s_all[g, color]) for color in range(3)], axis=0)
        out_ref[512:584, 128 * g : 128 * g + 128] = block.astype(jnp.bfloat16)
    for copy in started:
        copy.wait_send()


def score_kernel(x_ref, avg_ref, score_ref, final, gathered, products, flat_avg, score_row, sem):
    grp = lax.axis_index("grp")

    def f32(value):
        return value.astype(jnp.float32)

    def dot(a, b, dims=(((1,), (0,)), ((), ()))):
        return lax.dot_general(a, b, dims, preferred_element_type=jnp.float32)

    def matches(shape, row_of, lane_of):
        return jnp.where(row_of(iota(shape, 0)) == lane_of(iota(shape, 1)), 1.0, 0.0)

    def cos_at(k):
        size = jnp.abs(k - 32)
        return jnp.where(size == 32, 63, size)

    def sin_at(k):
        size = jnp.abs(k - 32)
        return jnp.where(size == 0, -1, jnp.where(size == 32, 64, size + 31))

    row = iota((128, 128), 0)
    lane = iota((128, 128), 1)
    ky = 2 * (row & 31) + ((row >> 5) & 1)
    ysel = jnp.where(
        row < 64,
        jnp.where(cos_at(ky) == lane, 1.0, 0.0),
        jnp.where(sin_at(ky) == lane, jnp.where(ky < 32, -1.0, 1.0), 0.0),
    ).astype(jnp.bfloat16)
    kx = lane & 63
    same = (row >> 6) == (lane >> 6)
    xc = jnp.where(same & (cos_at(kx) == (row & 63)), 1.0, 0.0)
    xs = jnp.where(same & (sin_at(kx) == (row & 63)), jnp.where(kx < 32, -1.0, 1.0), 0.0)
    xsel = jnp.concatenate([xc, xs], axis=1).astype(jnp.bfloat16)
    srow, slane = iota((32, 512), 0), iota((32, 512), 1)
    at = (srow & 7) - 1
    spot = jnp.where(
        ((srow >> 3) == (slane >> 7)) & (at >= 0) & (at < 2) & ((slane & 127) == at * 64), 1.0, 0.0
    ).astype(jnp.bfloat16)
    frow, flane = iota((32, 128), 0), iota((32, 128), 1)
    fy = f32(2 * frow + (flane >> 6) - 32)
    fx = f32((flane & 63) - 32)
    filt = jnp.exp(-(fy * fy + fx * fx) / (BAND * BAND / 2.0))
    bits = iota((8, 128), 1) - 65
    weight = jnp.where((bits >= 0) & (bits < 12), f32(1 << jnp.clip(bits, 0, 12)), 0.0)

    y = dot(ysel[:, :72], x_ref[512:584, 0:512]).astype(jnp.bfloat16)
    y = jnp.concatenate([y[:, 128 * g : 128 * g + 128] for g in range(4)], axis=0)
    z = dot(y, xsel)
    extra = jnp.concatenate([x_ref[576:584, 128 * g : 128 * g + 128] for g in range(4)], axis=0)
    side = dot(ysel, extra, (((1,), (1,)), ((), ()))).astype(jnp.bfloat16)
    side = dot(side, spot)
    half = iota((32, 128), 1) < 64
    for g in range(4):
        rc = z[128 * g : 128 * g + 128, :128]
        rs = z[128 * g : 128 * g + 128, 128:]
        sg = side[:, 128 * g : 128 * g + 128]
        members = jnp.sum(f32(x_ref[576:584, 128 * g : 128 * g + 128]) * weight, axis=1, keepdims=True)
        planes = (rc[:64] - rs[64:] + sg[64:], sg[:64] - rc[64:] - rs[:64])
        for j in range(2):
            scale = filt / (members[1 + j : 2 + j] + ridge)
            for p in range(2):
                even, odd = planes[p][:32], planes[p][32:]
                if j == 0:
                    odd = pltpu.roll(odd, 64, 1)
                else:
                    even = pltpu.roll(even, 64, 1)
                value = jnp.where(half, even, odd) * scale
                final[g, j, p] = value
                gathered[pl.ds(256 * p + 2 * g + j, 32, stride=8), :] = f32(
                    value.astype(jnp.bfloat16)
                )
    for t in range(32):
        for j in range(2):
            flat_avg[j, :, 128 * t : 128 * t + 128] = final[grp, j, :, t, :]
    copy = pltpu.make_async_copy(flat_avg, avg_ref, sem.at[0])
    copy.start()

    energy = jnp.zeros((8, 128), jnp.float32)
    inner = jnp.zeros((512, 16), jnp.float32)
    for t in range(0, 32, 2):
        sides = []
        for u in (t, t + 1):
            re = gathered[8 * u : 8 * u + 8, :]
            im = gathered[256 + 8 * u : 264 + 8 * u, :]
            energy += re * re + im * im
            sides.append(jnp.concatenate([re, im], axis=0).astype(jnp.bfloat16))
        inner += dot(
            x_ref[0:512, 128 * t : 128 * t + 256],
            jnp.concatenate(sides, axis=1),
            (((1,), (1,)), ((), ())),
        )
    products[0:512, 0:16] = inner
    both = products[pl.ds(0, 256, stride=2), :] + pltpu.roll(
        products[pl.ds(1, 256, stride=2), :], 120, 1
    )
    energy = jnp.sum(energy, axis=1, keepdims=True)
    score_row[...] = (both.T[:8] - 0.5 * energy) / BAND
    last = pltpu.make_async_copy(score_row, score_ref, sem.at[1])
    last.start()
    copy.wait()
    last.wait()


def scores_of(x):
    return pl.pallas_call(
        score_kernel,
        out_shape=(
            jax.ShapeDtypeStruct((2, 2, BAND * BAND), jnp.float32),
            jax.ShapeDtypeStruct((8, 256), jnp.float32),
        ),
        in_specs=[pl.BlockSpec(memory_space=pltpu.VMEM)],
        out_specs=(pl.BlockSpec(memory_space=pl.ANY),) * 2,
        scratch_shapes=[
            pltpu.VMEM((4, 2, 2, 32, 128), jnp.float32),
            pltpu.VMEM((528, 128), jnp.float32),
            pltpu.VMEM((528, 128), jnp.float32),
            pltpu.VMEM((2, 2, BAND * BAND), jnp.float32),
            pltpu.VMEM((8, 256), jnp.float32),
            pltpu.SemaphoreType.DMA((2,)),
        ],
        compiler_params=pltpu.CompilerParams(vmem_limit_bytes=8 << 20),
        name="scores_of",
    )(x)


def reduce_classes(acc, meta, next_block):
    vmem = pl.BlockSpec(memory_space=pltpu.VMEM)
    bf16 = jnp.bfloat16
    return pl.pallas_call(
        reduce_kernel,
        out_shape=pltpu.VMEM((592, 4096), bf16),
        in_specs=[vmem] * 3,
        out_specs=vmem,
        scratch_shapes=[
            pltpu.VMEM((64, PIX, 128), bf16),
            pltpu.VMEM((PIX, 128), jnp.float32),
            pltpu.VMEM((PIX, 128), jnp.float32),
            pltpu.VMEM((3, 1536, 128), jnp.float32),
            pltpu.VMEM((3, 1536, 128), bf16),
            pltpu.VMEM((3, 1536, 128), bf16),
            pltpu.VMEM((3, 1536, 128), bf16),
            pltpu.VMEM((3, 3, CHUNK, 128), bf16),
            pltpu.VMEM((3, 16, 24, 128), bf16),
            pltpu.VMEM((3, 15, 24, 128), bf16),
            pltpu.VMEM((4, 3, 24, 128), bf16),
            pltpu.VMEM((2 * PIX, 256), bf16),
            pltpu.SemaphoreType.DMA((3, 4)),
            pltpu.SemaphoreType.DMA((3, 4)),
            pltpu.SemaphoreType.DMA((3, 6)),
            pltpu.SemaphoreType.DMA((3, 6)),
            pltpu.SemaphoreType.DMA((3, 15)),
            pltpu.SemaphoreType.DMA((3, 15)),
            pltpu.SemaphoreType.DMA((3, 3)),
            pltpu.SemaphoreType.DMA((3, 3)),
        ],
        compiler_params=pltpu.CompilerParams(
            collective_id=0, has_side_effects=True, vmem_limit_bytes=24 << 20
        ),
        name="reduce_classes",
    )(acc, meta, next_block)


def body(images, shifts, class_ids, next_block):
    meta = jnp.concatenate([shifts.T, class_ids[None, :]], axis=0)
    return tuple(scores_of(reduce_classes(class_images(images, meta), meta, next_block)))


def solution(mesh):
    placed = (
        P(("dp", "grp"), None, None),
        P(("dp", "grp"), None),
        P(("dp", "grp")),
        P("grp", None, None),
    )
    return jax.shard_map(
        body,
        mesh=mesh,
        in_specs=placed,
        out_specs=(P(("dp", "grp"), None, None), P("dp", "grp")),
        check_vma=False,
    )
```
